256 devices in a mesh: gx: 4 (over z_hi), gy: 8 (over x, z_lo), gz: 8 (over y, core).
Axes of the slice: x: 4, y: 4, z: 8 (z_hi: 4, z_lo: 2; z = z_hi * 2 + z_lo), core: 2. Of those that a mesh axis runs over, the one named last changes fastest.
Arguments:
- weights: bfloat16 [32, 32, 32, 2, 8, 512], P('gx', 'gy', 'gz'), may hold values from -6 to 6
- angles: float32 [3, 32, 32, 32, 512], P(None, 'gx', 'gy', 'gz'), may hold values from -3.140625 to 3.140625
- translation: bfloat16 [8, 512, 512], replicated, may hold values from -0.09375 to 0.09375
Outputs:
- transformed: bfloat16 [32, 32, 32, 2, 8, 512], P('gx', 'gy', 'gz')
The draws below stay inside these ranges and needn't reach their ends.
All inputs are finite; a program needn't handle non-finite values.
Results may differ from the reference program's by a relative error of at most 0.025.
Values may be sent and summed in bfloat16 or wider, within the bound.
No kernel may reach another device: no remote copies, remote signals or barrier semaphores. Data moves between devices by JAX's collectives and lax.ppermute only.
A program may use at most 64 MiB of HBM per device.

```python
import jax
import jax.numpy as jnp
from jax import lax

PX = 32
PY = 32
PZ = 32
CHEB = 512
RHS = 8
LEVELS = 3


def block_scale(key, extent, cuts, smallest, top_value):
    def one(dim, blocks):
        heights = jax.random.uniform(jax.random.fold_in(jax.random.fold_in(key, 6), dim), (blocks,), jnp.float32, smallest / len(cuts), top_value / len(cuts))
        return jnp.repeat(jnp.exp(heights), extent[dim] // blocks).reshape((-1,) + (1,) * (len(extent) - dim - 1))

    level = one(*cuts[0])
    for cut in cuts[1:]:
        level = level * one(*cut)
    return level


def scatter_about(own_key, dims, scale, most, pieces=(), dtype=jnp.bfloat16):
    loudness = block_scale(own_key, dims, pieces, -0.22, 0.18) if pieces else 1.0
    array = jax.random.normal(own_key, dims, jnp.float32) * scale * loudness
    return jnp.minimum(jnp.maximum(array, -most), most).astype(dtype)


def setup_inputs(seed: int = 0) -> dict:
    streams_of = jax.random.split(jax.random.key(seed), 4)
    weights = scatter_about(streams_of[0], (PX, PY, PZ, 2, RHS, CHEB), 1.0, 6.0, ((0, 4), (1, 8), (2, 8)))
    angles = jnp.clip(jax.random.uniform(streams_of[1], (LEVELS, PX, PY, PZ, CHEB), jnp.float32, -3.140625, 3.140625), -3.140625, 3.140625)
    translation = scatter_about(streams_of[2], (8, CHEB, CHEB), (8 * CHEB) ** -0.5, 0.09375)
    return {"weights": weights, "angles": angles, "translation": translation}


def rotate_phase(current, angle):
    real_part = current[:, :, :, 0].astype(jnp.float32)
    imag_part = current[:, :, :, 1].astype(jnp.float32)
    cosine = jnp.cos(angle)[:, :, :, None, :]
    sine = jnp.sin(angle)[:, :, :, None, :]
    rotated_re = real_part * cosine - imag_part * sine
    rotated_im = real_part * sine + imag_part * cosine
    return jnp.stack([rotated_re, rotated_im], axis=3).astype(jnp.bfloat16)


def fold_local(child_terms, dim_pos, low_span):
    dims_shape = child_terms.shape
    count = dims_shape[dim_pos]
    split = child_terms.reshape(dims_shape[:dim_pos] + (count // (2 * low_span), 2, low_span) + dims_shape[dim_pos + 1:])
    first = jnp.take(split, 0, axis=dim_pos + 1).astype(jnp.float32)
    second = jnp.take(split, 1, axis=dim_pos + 1).astype(jnp.float32)
    added = (first + second).astype(jnp.bfloat16)
    return added.reshape(dims_shape[:dim_pos] + (count // 2,) + dims_shape[dim_pos + 1:])


def insert_bit(lower, upper, dim_pos, low_span):
    dims_shape = lower.shape
    count = dims_shape[dim_pos]
    inner_shape = dims_shape[:dim_pos] + (count // low_span, low_span) + dims_shape[dim_pos + 1:]
    stacked = jnp.stack([lower.reshape(inner_shape), upper.reshape(inner_shape)], axis=dim_pos + 1)
    return stacked.reshape(dims_shape[:dim_pos] + (2 * count,) + dims_shape[dim_pos + 1:])


def translate_all(summed, translation, local_dims, chosen_bits):
    if not local_dims:
        orient = 4 * chosen_bits[0] + 2 * chosen_bits[1] + chosen_bits[2]
        matrix = lax.dynamic_index_in_dim(translation, orient, 0, keepdims=False)
        rows = summed.reshape(-1, summed.shape[-1])
        result = jnp.dot(rows, matrix, preferred_element_type=jnp.float32)
        return result.astype(jnp.bfloat16).reshape(summed.shape)
    dim_pos, low_span = local_dims[0]
    halves = []
    for t in (0, 1):
        picked = dict(chosen_bits)
        picked[dim_pos] = t
        halves.append(translate_all(summed, translation, local_dims[1:], picked))
    return insert_bit(halves[0], halves[1], dim_pos, low_span)


def reference(weights, angles, translation):
    current = weights
    size_list = (PX, PY, PZ)
    for level_idx in range(LEVELS):
        child_terms = rotate_phase(current, angles[level_idx])
        local_dims = []
        for d in range(3):
            low_span = 2 ** (size_list[d].bit_length() - 2 - level_idx)
            child_terms = fold_local(child_terms, d, low_span)
            local_dims.append((d, low_span))
        current = translate_all(child_terms, translation, local_dims, dict())
    return current
```

```python
import jax
import jax.numpy as jnp
import numpy as np
from jax import lax
from jax.experimental import pallas as pl
from jax.experimental.pallas import tpu as pltpu
from jax.sharding import Mesh
from jax.sharding import PartitionSpec as P

BITS = ("x4", "x3", "y4", "y3", "y2", "z4", "z3", "z2")
CHEB = 512
HALF = 256
BF = jnp.bfloat16
F32 = jnp.float32

SIN = (1.0, -0.1666666567325592, 0.00833332072943449, -0.00019840527966152877, 2.753572516667191e-06,
       -2.472758353633253e-08, 1.3608578153245787e-10)
COS = (1.0, -0.49999988079071045, 0.04166648909449577, -0.0013887794921174645, 2.4769700758042745e-05,
       -2.707722615014063e-07, 1.7238451777146224e-09)


def sin_cos(angle):
    square = angle * angle
    sine, cosine = jnp.full_like(square, SIN[-1]), jnp.full_like(square, COS[-1])
    for s, c in zip(SIN[-2::-1], COS[-2::-1]):
        sine, cosine = sine * square + s, cosine * square + c
    return sine * angle, cosine


def selection(source, count):
    source = np.asarray(source).reshape(-1)
    matrix = np.zeros((source.size, count), np.float32)
    matrix[np.arange(source.size), source] = 1
    return matrix


def rows(dims, order):
    return np.arange(int(np.prod(dims))).reshape(dims).transpose(order)


MIX = selection(rows((2, 8, 2, 4, 2), (1, 3, 0, 2, 4)), 256)
SEND_PHASE = selection(rows((2, 2, 2, 16), (3, 1, 2, 0)), 128)
ENTER = selection(rows((8, 4, 2, 2, 2), (0, 3, 4, 1, 2)), 256)
TURN = selection(rows((8, 2, 2, 8), (3, 1, 2, 0)), 256)
LEAVE = selection(rows((2, 2, 2, 2, 2, 2), (4, 5, 3, 1, 2, 0)), 64)


def phase_picks():
    first, second = [], []
    at = np.arange(256).reshape(4, 8, 2, 2, 2)
    for own in range(4):
        near = at[[yz ^ own for yz in range(4)]]
        first.append(selection(near[:, :, 0].transpose(3, 1, 0, 2), 256))
        second.append(selection(near[:, :, 1].transpose(3, 0, 2, 1), 256))
    return np.stack(first), np.stack(second)


def final_picks():
    at = np.arange(256).reshape(4, 8, 2, 2, 2)
    return np.stack(
        [
            selection(at[[yz ^ own for yz in range(4)]].transpose(4, 1, 2, 0, 3), 256)
            for own in range(4)
        ]
    )


FIRST, SECOND = phase_picks()
FINAL = final_picks()


def dot(a, b):
    return jnp.dot(a, b, preferred_element_type=F32)


def params():
    return pltpu.CompilerParams(vmem_limit_bytes=48 * 1024 * 1024)


def rotate_kernel(place, w_ref, a_ref, mix_ref, order_ref, send0, keep0, send1, keep1, phases, angle, mixed):
    step = pl.program_id(0)
    for level in range(3):
        for x2 in range(2):
            for y in range(4):
                angle[level, x2, 4 * y : 4 * y + 4, :] = a_ref[level, x2, 0, y]
    for x2 in range(2):
        sine, cosine = sin_cos(angle[0, x2])
        angle[0, x2] = sine
        for low in range(16):
            block = w_ref[x2, 0, 16 * low : 16 * low + 16, :].astype(F32)
            re, im = block[:8], block[8:]
            s, c = angle[0, x2, low : low + 1, :], cosine[low : low + 1]
            turned = jnp.concatenate([re * c - im * s, re * s + im * c], axis=0)
            at = 128 * x2 + 16 * (low % 8)
            mixed[low // 8, at : at + 16, :] = turned.astype(BF)
    far = angle[1:3].reshape(64, CHEB).astype(BF)
    far = jnp.concatenate([far[:, :HALF], far[:, HALF:]], axis=0)
    far = dot(order_ref[...], far).astype(BF)
    for high in range(2):
        phases[high, 0] = far[64 * high : 64 * high + 64]
    first = dot(mix_ref[...], mixed[0]).astype(BF)
    second = dot(mix_ref[...], mixed[1]).astype(BF)

    @pl.when(step < 2)
    def _():
        send0[0] = first

    @pl.when(step >= 2)
    def _():
        keep0[0] = first

    @pl.when(step % 2 == 0)
    def _():
        send1[0] = second

    @pl.when(step % 2 == 1)
    def _():
        keep1[0] = second


def rotate(place, weights, angles):
    def block(i, place):
        return (place[0] ^ (1 - i // 2)) * 2 + (place[1] ^ (1 - i % 2))

    piece = jax.ShapeDtypeStruct((2, 256, CHEB), BF)
    spec = pltpu.PrefetchScalarGridSpec(
        num_scalar_prefetch=1,
        grid=(4,),
        in_specs=[
            pl.BlockSpec((2, 1, 256, CHEB), lambda i, p: (0, block(i, p), 0, 0)),
            pl.BlockSpec((3, 2, 1, 4, 4, CHEB), lambda i, p: (0, 0, block(i, p), 0, 0, 0)),
            pl.BlockSpec((256, 256), lambda i, p: (0, 0)),
            pl.BlockSpec((128, 128), lambda i, p: (0, 0)),
        ],
        out_specs=[
            pl.BlockSpec((1, 256, CHEB), lambda i, p: (jnp.minimum(i, 1), 0, 0)),
            pl.BlockSpec((1, 256, CHEB), lambda i, p: (jnp.maximum(i - 2, 0), 0, 0)),
            pl.BlockSpec((1, 256, CHEB), lambda i, p: (i // 2, 0, 0)),
            pl.BlockSpec((1, 256, CHEB), lambda i, p: (i // 2, 0, 0)),
            pl.BlockSpec((2, 1, 64, HALF), lambda i, p: (0, block(i, p), 0, 0)),
        ],
        scratch_shapes=[pltpu.VMEM((3, 2, 16, CHEB), F32), pltpu.VMEM((2, 256, CHEB), BF)],
    )
    return pl.pallas_call(
        rotate_kernel,
        grid_spec=spec,
        out_shape=[piece] * 4 + [jax.ShapeDtypeStruct((2, 4, 64, HALF), BF)],
        compiler_params=params(),
        name="rotate",
    )(
        place,
        weights.reshape(2, 4, 256, CHEB),
        angles.reshape(3, 2, 4, 4, 4, CHEB),
        jnp.asarray(MIX, BF),
        jnp.asarray(SEND_PHASE, BF),
    )


def levels_kernel(place, x_ref, t_ref, *refs):
    near1, near2 = refs[0:4], refs[4:8]
    enter_ref, first_ref, second_ref, turn_ref, leave_ref, out_ref, left, middle, product, angle = refs[8:]
    step = pl.program_id(0)

    @pl.when(step == 0)
    def _():
        total = (x_ref[0].astype(F32) + x_ref[1].astype(F32)).astype(BF)
        left[...] = dot(enter_ref[...], total).astype(BF)

    @pl.when(step == 8)
    def _():
        left[...] = dot(turn_ref[...], middle[...]).astype(BF)

    @pl.when(step < 8)
    def _():
        held = jnp.concatenate([r[0] for r in near1], axis=0)
        angle[...] = dot(first_ref[0], held)

    @pl.when(step >= 8)
    def _():
        held = jnp.concatenate([r[...].astype(F32).reshape(64, HALF) for r in near2], axis=0)
        angle[...] = dot(second_ref[0], held.astype(BF))

    product[...] = dot(left[...], t_ref[0])
    total = [jnp.zeros((8, CHEB), F32)] * 4
    for outer in range(8):
        at = 8 * outer
        theta = jnp.concatenate([angle[at : at + 8], angle[64 + at : 72 + at]], axis=1)
        sine, cosine = sin_cos(theta)
        at = 32 * outer
        for r in range(2):
            re = product[at + 8 * r : at + 8 * r + 8]
            im = product[at + 16 + 8 * r : at + 24 + 8 * r]
            total[r] = total[r] + (re * cosine - im * sine)
            total[2 + r] = total[2 + r] + (re * sine + im * cosine)
    summed = jnp.concatenate(total, axis=0)

    @pl.when(step < 8)
    def _():
        middle[pl.ds(pl.multiple_of(step * 32, 32), 32), :] = summed.astype(BF)

    @pl.when(step >= 8)
    def _():
        value = summed.astype(BF)
        value = jnp.concatenate([value[:, :HALF], value[:, HALF:]], axis=0)
        value = dot(leave_ref[...], value)
        for t4 in range(8):
            out_ref[t4] = value[8 * t4 : 8 * t4 + 8].astype(BF)


def levels(place, share, translation, near):
    def const(*shape):
        return pl.BlockSpec(shape, lambda i, p: (0,) * len(shape))

    def own(*shape):
        return pl.BlockSpec((1, *shape), lambda i, p: (p[2],) + (0,) * len(shape))

    spec = pltpu.PrefetchScalarGridSpec(
        num_scalar_prefetch=1,
        grid=(16,),
        in_specs=[const(2, 256, CHEB), pl.BlockSpec((1, CHEB, CHEB), lambda i, p: (i % 8, 0, 0))]
        + [pl.BlockSpec((1, 64, HALF), lambda i, p: (jnp.minimum(i, 7), 0, 0))] * 4
        + [pl.BlockSpec((8, 8, HALF), lambda i, p: (0, jnp.maximum(i - 8, 0), 0))] * 4
        + [const(256, 256), own(128, 256), own(128, 256), const(256, 256), const(64, 64)],
        out_specs=pl.BlockSpec((8, 8, HALF), lambda i, p: (0, jnp.maximum(i - 8, 0), 0)),
        scratch_shapes=[
            pltpu.VMEM((256, CHEB), BF),
            pltpu.VMEM((256, CHEB), BF),
            pltpu.VMEM((256, CHEB), F32),
            pltpu.VMEM((128, HALF), F32),
        ],
    )
    return pl.pallas_call(
        levels_kernel,
        grid_spec=spec,
        out_shape=jax.ShapeDtypeStruct((8, 64, HALF), BF),
        compiler_params=params(),
        name="levels",
    )(
        place,
        share,
        translation,
        *near,
        *near,
        jnp.asarray(ENTER, BF),
        jnp.asarray(FIRST, BF),
        jnp.asarray(SECOND, BF),
        jnp.asarray(TURN, BF),
        jnp.asarray(LEAVE, BF),
    )


def final_kernel(place, n0, n1, n2, n3, pick_ref, t_ref, out_ref, left):
    for high in range(2):
        held = jnp.concatenate([r[64 * high : 64 * high + 64] for r in (n0, n1, n2, n3)], axis=0)
        value = dot(pick_ref[0], held)
        value = jnp.concatenate([value[:128], value[128:]], axis=1)
        left[128 * high : 128 * high + 128, :] = value.astype(BF)
    for x2 in range(2):
        out_ref[x2, 0] = dot(left[...], t_ref[x2, 0]).astype(BF)


def final(place, near, translation):
    spec = pltpu.PrefetchScalarGridSpec(
        num_scalar_prefetch=1,
        grid=(4,),
        in_specs=[pl.BlockSpec((128, HALF), lambda i, p: (i, 0))] * 4
        + [
            pl.BlockSpec((1, 256, 256), lambda i, p: (p[2], 0, 0)),
            pl.BlockSpec((2, 1, CHEB, CHEB), lambda i, p: (0, p[2], 0, 0)),
        ],
        out_specs=pl.BlockSpec((2, 1, 256, CHEB), lambda i, p: (0, i, 0, 0)),
        scratch_shapes=[pltpu.VMEM((256, CHEB), BF)],
    )
    return pl.pallas_call(
        final_kernel,
        grid_spec=spec,
        out_shape=jax.ShapeDtypeStruct((2, 4, 256, CHEB), BF),
        compiler_params=params(),
        name="final",
    )(place, *near, jnp.asarray(FINAL, BF), translation.reshape(2, 4, CHEB, CHEB))


def swap(value, axis):
    return lax.ppermute(value, axis, [(0, 1), (1, 0)])


def add(a, b):
    return (a.astype(F32) + b.astype(F32)).astype(BF)


def four(value):
    other = swap(value, "y2")
    return value, swap(value, "z2"), other, swap(other, "z2")


def exchange(value, axes):
    return lax.all_to_all(value, axes, split_axis=0, concat_axis=0, tiled=True)


def shards(weights, angles, translation):
    bit = lax.axis_index
    place = jnp.stack([bit("y4"), bit("z4"), 2 * bit("y2") + bit("z2")]).astype(jnp.int32)
    send0, keep0, send1, keep1, phases = rotate(place, weights, angles)
    come0, come1 = swap(send0, "y4"), swap(send1, "z4")
    again0, again1 = add(keep0[0], come0[0]), add(keep1[0], come1[0])
    come0, again0 = add(keep0[1], come0[1]), swap(again0, "z4")
    come1, again1 = add(keep1[1], come1[1]), swap(again1, "y4")
    share = jnp.stack([add(come0, again0), add(come1, again1)])
    share = exchange(share.reshape(64, 8, CHEB), ("x4", "x3", "y3", "z3", "y2", "z2"))
    phases = exchange(phases.reshape(64, 8, HALF), ("x4", "y4", "z4", "x3", "y3", "z3"))
    near = four(phases.reshape(8, 64, HALF))
    done = levels(place, share.reshape(2, 256, CHEB), translation, near)
    done = exchange(done.reshape(64, 8, HALF), ("y4", "z4", "x4", "x3", "y3", "z3"))
    near = four(done.reshape(512, HALF))
    return final(place, near, translation).reshape(weights.shape)


def solution(mesh):
    fine = Mesh(mesh.devices.reshape((2,) * len(BITS)), BITS)
    x, y, z = BITS[:2], BITS[2:5], BITS[5:]
    return jax.shard_map(
        shards,
        mesh=fine,
        in_specs=(P(x, y, z, None, None, None), P(None, x, y, z, None), P()),
        out_specs=P(x, y, z, None, None, None),
        check_vma=False,
    )
```

```python
import jax
import jax.numpy as jnp
import numpy as np
from jax import lax
from jax.experimental import pallas as pl
from jax.experimental.pallas import tpu as pltpu
from jax.sharding import Mesh
from jax.sharding import PartitionSpec as P

BITS = ("x4", "x3", "y4", "y3", "y2", "z4", "z3", "z2")
CHEB = 512
HALF = 256
BF = jnp.bfloat16
F32 = jnp.float32

SIN = (1.0, -0.1666666567325592, 0.00833332072943449, -0.00019840527966152877, 2.753572516667191e-06,
       -2.472758353633253e-08, 1.3608578153245787e-10)
COS = (1.0, -0.49999988079071045, 0.04166648909449577, -0.0013887794921174645, 2.4769700758042745e-05,
       -2.707722615014063e-07, 1.7238451777146224e-09)


def sin_cos(angle):
    square = angle * angle
    sine, cosine = jnp.full_like(square, SIN[-1]), jnp.full_like(square, COS[-1])
    for s, c in zip(SIN[-2::-1], COS[-2::-1]):
        sine, cosine = sine * square + s, cosine * square + c
    return sine * angle, cosine


def selection(source, count):
    source = np.asarray(source).reshape(-1)
    matrix = np.zeros((source.size, count), np.float32)
    matrix[np.arange(source.size), source] = 1
    return matrix


def rows(dims, order):
    return np.arange(int(np.prod(dims))).reshape(dims).transpose(order)


MIX = selection(rows((2, 8, 2, 4, 2), (1, 3, 0, 2, 4)), 256)
SEND_PHASE = selection(rows((2, 2, 2, 16), (3, 1, 2, 0)), 128)
ENTER = selection(rows((8, 4, 2, 2, 2), (0, 3, 4, 1, 2)), 256)
TURN = selection(rows((8, 2, 2, 8), (3, 1, 2, 0)), 256)
LEAVE = selection(rows((2, 2, 2, 2, 2, 2), (4, 5, 3, 1, 2, 0)), 64)


def phase_picks():
    first, second = [], []
    at = np.arange(256).reshape(4, 8, 2, 2, 2)
    for own in range(4):
        near = at[[yz ^ own for yz in range(4)]]
        first.append(selection(near[:, :, 0].transpose(3, 1, 0, 2), 256))
        second.append(selection(near[:, :, 1].transpose(3, 0, 2, 1), 256))
    return np.stack(first), np.stack(second)


def final_picks():
    at = np.arange(256).reshape(4, 8, 2, 2, 2)
    return np.stack(
        [
            selection(at[[yz ^ own for yz in range(4)]].transpose(4, 1, 2, 0, 3), 256)
            for own in range(4)
        ]
    )


FIRST, SECOND = phase_picks()
FINAL = final_picks()


def dot(a, b):
    return jnp.dot(a, b, preferred_element_type=F32)


def in_hbm(value):
    return pltpu.with_memory_space_constraint(value, pltpu.HBM)


def params(mebibytes):
    return pltpu.CompilerParams(vmem_limit_bytes=mebibytes * 1024 * 1024)


def rotate_half(w_ref, a_ref, mix_ref, first, second, angle, mixed):
    step = pl.program_id(0)
    for x2 in range(2):
        for y in range(2):
            angle[x2, 4 * y : 4 * y + 4, :] = a_ref[0, x2, 0, y]
        sine, cosine = sin_cos(angle[x2])
        for low in range(8):
            block = w_ref[x2, 0, 16 * low : 16 * low + 16, :].astype(F32)
            re, im = block[:8], block[8:]
            s, c = sine[low : low + 1], cosine[low : low + 1]
            turned = jnp.concatenate([re * c - im * s, re * s + im * c], axis=0)
            at = 128 * x2 + 16 * low
            mixed[at : at + 16, :] = turned.astype(BF)
    value = dot(mix_ref[...], mixed[...]).astype(BF)

    @pl.when(step < 2)
    def _():
        first[0] = value

    @pl.when(step >= 2)
    def _():
        second[0] = value


def send_kernel(place, w_ref, a_ref, mix_ref, first, second, angle, mixed):
    rotate_half(w_ref, a_ref, mix_ref, first, second, angle, mixed)


def keep_kernel(place, w_ref, a_ref, mix_ref, a1_ref, a2_ref, order_ref, first, second, phases, angle, mixed, far):
    rotate_half(w_ref, a_ref, mix_ref, first, second, angle, mixed)
    for level, ref in enumerate((a1_ref, a2_ref)):
        for x2 in range(2):
            for y in range(4):
                at = 32 * level + 16 * x2 + 4 * y
                far[at : at + 4, :] = ref[0, x2, 0, y]
    value = far[...].astype(BF)
    value = jnp.concatenate([value[:, :HALF], value[:, HALF:]], axis=0)
    value = dot(order_ref[...], value).astype(BF)
    for high in range(2):
        phases[high, 0] = value[64 * high : 64 * high + 64]


def rotate(place, weights, angles, keep):
    def block(j, place):
        if keep:
            y, z = jnp.where(j == 2, 0, 1), jnp.where(j == 0, 0, 1)
        else:
            y, z = jnp.where(j == 3, 1, 0), jnp.where(j == 1, 1, 0)
        return (place[0] ^ (1 - y)) * 2 + (place[1] ^ (1 - z))

    piece = jax.ShapeDtypeStruct((2, 256, CHEB), BF)
    in_specs = [
        pl.BlockSpec((2, 1, 128, CHEB), lambda j, p: (0, block(j, p), j // 2, 0)),
        pl.BlockSpec((1, 2, 1, 2, 4, CHEB), lambda j, p: (0, 0, block(j, p), j // 2, 0, 0)),
        pl.BlockSpec((256, 256), lambda j, p: (0, 0)),
    ]
    out_specs = [
        pl.BlockSpec((1, 256, CHEB), lambda j, p: (jnp.minimum(j, 1), 0, 0)),
        pl.BlockSpec((1, 256, CHEB), lambda j, p: (jnp.maximum(j - 2, 0), 0, 0)),
    ]
    out_shape = [piece] * 2
    scratch = [pltpu.VMEM((2, 8, CHEB), F32), pltpu.VMEM((256, CHEB), BF)]
    args = [weights, angles, jnp.asarray(MIX, BF)]
    if keep:
        in_specs += [
            pl.BlockSpec((1, 2, 1, 4, 4, CHEB), lambda j, p: (1, 0, j, 0, 0, 0)),
            pl.BlockSpec((1, 2, 1, 4, 4, CHEB), lambda j, p: (2, 0, j, 0, 0, 0)),
            pl.BlockSpec((128, 128), lambda j, p: (0, 0)),
        ]
        out_specs.append(pl.BlockSpec((2, 1, 64, HALF), lambda j, p: (0, j, 0, 0)))
        out_shape.append(jax.ShapeDtypeStruct((2, 4, 64, HALF), BF))
        scratch.append(pltpu.VMEM((64, CHEB), F32))
        args += [angles, angles, jnp.asarray(SEND_PHASE, BF)]
    spec = pltpu.PrefetchScalarGridSpec(
        num_scalar_prefetch=1, grid=(4,), in_specs=in_specs, out_specs=out_specs, scratch_shapes=scratch
    )
    return pl.pallas_call(
        keep_kernel if keep else send_kernel,
        grid_spec=spec,
        out_shape=out_shape,
        compiler_params=params(12),
        name="rotate_kept" if keep else "rotate_sent",
    )(place, *args)


def add(a, b):
    return (a.astype(F32) + b.astype(F32)).astype(BF)


def sum_kernel(keep0, come0, again0, keep1, come1, again1, out_ref):
    for half, (kept, come, again) in enumerate(((keep0, come0, again0), (keep1, come1, again1))):
        out_ref[half] = add(add(kept[1], come[1]), again[...])


def sums(*args):
    return pl.pallas_call(
        sum_kernel,
        out_shape=jax.ShapeDtypeStruct((2, 256, CHEB), BF),
        in_specs=[pl.BlockSpec(memory_space=pltpu.VMEM)] * 6,
        out_specs=pl.BlockSpec(memory_space=pltpu.VMEM),
        compiler_params=params(8),
        name="sums",
    )(*args)


def trig_kernel(place, *refs):
    near1, near2 = refs[0:4], refs[4:8]
    first_ref, second_ref, out_ref, angle = refs[8:]
    step = pl.program_id(0)

    @pl.when(step < 8)
    def _():
        held = jnp.concatenate([r[0] for r in near1], axis=0)
        angle[...] = dot(first_ref[0], held)

    @pl.when(step >= 8)
    def _():
        held = jnp.concatenate([r[...].astype(F32).reshape(64, HALF) for r in near2], axis=0)
        angle[...] = dot(second_ref[0], held.astype(BF))

    for half in range(2):
        for at in range(0, 64, 16):
            sine, cosine = sin_cos(angle[64 * half + at : 64 * half + at + 16])
            out_ref[0, 0, at : at + 16, HALF * half : HALF * half + HALF] = sine
            out_ref[0, 1, at : at + 16, HALF * half : HALF * half + HALF] = cosine


def trig(place, near):
    def own(*shape):
        return pl.BlockSpec((1, *shape), lambda i, p: (p[2],) + (0,) * len(shape))

    spec = pltpu.PrefetchScalarGridSpec(
        num_scalar_prefetch=1,
        grid=(16,),
        in_specs=[pl.BlockSpec((1, 64, HALF), lambda i, p: (jnp.minimum(i, 7), 0, 0))] * 4
        + [pl.BlockSpec((8, 8, HALF), lambda i, p: (0, jnp.maximum(i - 8, 0), 0))] * 4
        + [own(128, 256), own(128, 256)],
        out_specs=pl.BlockSpec((1, 2, 64, CHEB), lambda i, p: (i, 0, 0, 0)),
        scratch_shapes=[pltpu.VMEM((128, HALF), F32)],
    )
    return pl.pallas_call(
        trig_kernel,
        grid_spec=spec,
        out_shape=pltpu.HBM((16, 2, 64, CHEB), F32),
        compiler_params=params(10),
        name="trig",
    )(place, *near, *near, jnp.asarray(FIRST, BF), jnp.asarray(SECOND, BF))


def levels_kernel(x_ref, t_ref, trig_ref, enter_ref, turn_ref, leave_ref, out_ref, left, middle, even, odd):
    step = pl.program_id(0)

    @pl.when(step == 0)
    def _():
        total = (x_ref[0].astype(F32) + x_ref[1].astype(F32)).astype(BF)
        left[...] = dot(enter_ref[...], total).astype(BF)

    @pl.when(step == 2)
    def _():
        left[...] = dot(turn_ref[...], middle[...]).astype(BF)

    def turn_and_sum(product, at):
        total = [jnp.zeros((8, CHEB), F32)] * 4
        for outer in range(8):
            sine = trig_ref[at, 0, 8 * outer : 8 * outer + 8, :]
            cosine = trig_ref[at, 1, 8 * outer : 8 * outer + 8, :]
            for r in range(2):
                row = 32 * outer + 8 * r
                re = product[row : row + 8, :]
                im = product[row + 16 : row + 24, :]
                total[r] = total[r] + (re * cosine - im * sine)
                total[2 + r] = total[2 + r] + (re * sine + im * cosine)
        return jnp.concatenate(total, axis=0).astype(BF)

    def four_orientations(put):
        even[...] = dot(left[...], t_ref[0])
        for t in range(4):
            if t < 3:
                (odd, even)[t % 2][...] = dot(left[...], t_ref[t + 1])
            put(t, turn_and_sum((even, odd)[t % 2], t))

    @pl.when(step < 2)
    def _():
        def put(t, value):
            row = pl.multiple_of(128 * step + 32 * t, 32)
            middle[pl.ds(row, 32), :] = value

        four_orientations(put)

    @pl.when(step >= 2)
    def _():
        def put(t, value):
            value = jnp.concatenate([value[:, :HALF], value[:, HALF:]], axis=0)
            value = dot(leave_ref[...], value)
            for t4 in range(8):
                out_ref[t4, t] = value[8 * t4 : 8 * t4 + 8].astype(BF)

        four_orientations(put)


def levels(share, translation, waves):
    def const(*shape):
        return pl.BlockSpec(shape, lambda i: (0,) * len(shape))

    return pl.pallas_call(
        levels_kernel,
        grid=(4,),
        out_shape=jax.ShapeDtypeStruct((8, 8, 8, HALF), BF),
        in_specs=[
            const(2, 256, CHEB),
            pl.BlockSpec((4, CHEB, CHEB), lambda i: (i % 2, 0, 0)),
            pl.BlockSpec((4, 2, 64, CHEB), lambda i: (i, 0, 0, 0)),
            const(256, 256),
            const(256, 256),
            const(64, 64),
        ],
        out_specs=pl.BlockSpec((8, 4, 8, HALF), lambda i: (0, jnp.maximum(i - 2, 0), 0, 0)),
        scratch_shapes=[
            pltpu.VMEM((256, CHEB), BF),
            pltpu.VMEM((256, CHEB), BF),
            pltpu.VMEM((256, CHEB), F32),
            pltpu.VMEM((256, CHEB), F32),
        ],
        compiler_params=params(20),
        name="levels",
    )(share, in_hbm(translation), in_hbm(waves), jnp.asarray(ENTER, BF), jnp.asarray(TURN, BF), jnp.asarray(LEAVE, BF))


def final_kernel(place, n0, n1, n2, n3, pick_ref, t_ref, out_ref, left):
    for high in range(2):
        held = jnp.concatenate([r[64 * high : 64 * high + 64] for r in (n0, n1, n2, n3)], axis=0)
        value = dot(pick_ref[0], held)
        value = jnp.concatenate([value[:128], value[128:]], axis=1)
        left[128 * high : 128 * high + 128, :] = value.astype(BF)
    for x2 in range(2):
        out_ref[x2, 0] = dot(left[...], t_ref[4 * x2 + place[2]]).astype(BF)


def final(place, near, translation):
    spec = pltpu.PrefetchScalarGridSpec(
        num_scalar_prefetch=1,
        grid=(4,),
        in_specs=[pl.BlockSpec((128, HALF), lambda i, p: (i, 0))] * 4
        + [
            pl.BlockSpec((1, 256, 256), lambda i, p: (p[2], 0, 0)),
            pl.BlockSpec(memory_space=pltpu.VMEM),
        ],
        out_specs=pl.BlockSpec((2, 1, 256, CHEB), lambda i, p: (0, i, 0, 0)),
        scratch_shapes=[pltpu.VMEM((256, CHEB), BF)],
    )
    return pl.pallas_call(
        final_kernel,
        grid_spec=spec,
        out_shape=jax.ShapeDtypeStruct((2, 4, 256, CHEB), BF),
        compiler_params=params(14),
        name="final",
    )(place, *near, jnp.asarray(FINAL, BF), translation)


def swap(value, axis):
    return lax.ppermute(value, axis, [(0, 1), (1, 0)])


def four(value):
    other = swap(value, "y2")
    return value, swap(value, "z2"), other, swap(other, "z2")


def exchange(value, axes):
    return lax.all_to_all(value, axes, split_axis=0, concat_axis=0, tiled=True)


def shards(weights, angles, translation):
    bit = lax.axis_index
    place = jnp.stack([bit("y4"), bit("z4"), 2 * bit("y2") + bit("z2")]).astype(jnp.int32)
    shape = weights.shape
    weights = in_hbm(weights.reshape(2, 4, 256, CHEB))
    angles = in_hbm(angles.reshape(3, 2, 4, 4, 4, CHEB))
    send0, send1 = rotate(place, weights, angles, False)
    come0, come1 = swap(send0, "y4"), swap(send1, "z4")
    keep0, keep1, phases = rotate(place, weights, angles, True)
    phases = exchange(phases.reshape(64, 8, HALF), ("x4", "y4", "z4", "x3", "y3", "z3"))
    again0, again1 = add(keep0[0], come0[0]), add(keep1[0], come1[0])
    phases, _, _ = lax.optimization_barrier((phases, again0, again1))
    near = four(phases.reshape(8, 64, HALF))
    again0, again1 = swap(again0, "z4"), swap(again1, "y4")
    share = sums(keep0, come0, again0, keep1, come1, again1)
    share = exchange(share.reshape(64, 8, CHEB), ("x4", "x3", "y3", "z3", "y2", "z2"))
    waves = trig(place, near)
    done = levels(share.reshape(2, 256, CHEB), translation, waves)
    done = exchange(done.reshape(64, 8, HALF), ("y4", "z4", "x4", "x3", "y3", "z3"))
    near = four(done.reshape(512, HALF))
    return final(place, near, translation).reshape(shape)


def solution(mesh):
    fine = Mesh(mesh.devices.reshape((2,) * len(BITS)), BITS)
    x, y, z = BITS[:2], BITS[2:5], BITS[5:]
    return jax.shard_map(
        shards,
        mesh=fine,
        in_specs=(P(x, y, z, None, None, None), P(None, x, y, z, None), P()),
        out_specs=P(x, y, z, None, None, None),
        check_vma=False,
    )
```

```python
import jax
import jax.numpy as jnp
import numpy as np
from jax import lax
from jax.experimental import pallas as pl
from jax.experimental.pallas import tpu as pltpu
from jax.sharding import Mesh
from jax.sharding import PartitionSpec as P

BITS = ("x4", "x3", "y4", "y3", "y2", "z4", "z3", "z2")
CHEB = 512
HALF = 256
BF = jnp.bfloat16
F32 = jnp.float32

SIN = (1.0, -0.1666666567325592, 0.00833332072943449, -0.00019840527966152877, 2.753572516667191e-06,
       -2.472758353633253e-08, 1.3608578153245787e-10)
COS = (1.0, -0.49999988079071045, 0.04166648909449577, -0.0013887794921174645, 2.4769700758042745e-05,
       -2.707722615014063e-07, 1.7238451777146224e-09)


def sin_cos(angle):
    square = angle * angle
    sine, cosine = jnp.full_like(square, SIN[-1]), jnp.full_like(square, COS[-1])
    for s, c in zip(SIN[-2::-1], COS[-2::-1]):
        sine, cosine = sine * square + s, cosine * square + c
    return sine * angle, cosine


def selection(source, count):
    source = np.asarray(source).reshape(-1)
    matrix = np.zeros((source.size, count), np.float32)
    matrix[np.arange(source.size), source] = 1
    return matrix


def rows(dims, order):
    return np.arange(int(np.prod(dims))).reshape(dims).transpose(order)


MIX = selection(rows((2, 8, 2, 4, 2), (1, 3, 0, 2, 4)), 256)
SEND_PHASE = selection(rows((2, 2, 2, 16), (3, 1, 2, 0)), 128)
ENTER = selection(rows((8, 4, 2, 2, 2), (0, 3, 4, 1, 2)), 256)
TURN = selection(rows((8, 2, 2, 8), (3, 1, 2, 0)), 256)
LEAVE = selection(rows((2, 2, 2, 2, 2, 2), (4, 5, 3, 1, 2, 0)), 64)


def phase_picks():
    first, second = [], []
    at = np.arange(256).reshape(4, 8, 2, 2, 2)
    for own in range(4):
        near = at[[yz ^ own for yz in range(4)]]
        first.append(selection(near[:, :, 0].transpose(3, 1, 0, 2), 256))
        second.append(selection(near[:, :, 1].transpose(3, 0, 2, 1), 256))
    return np.stack(first), np.stack(second)


def final_picks():
    at = np.arange(256).reshape(4, 8, 2, 2, 2)
    return np.stack(
        [
            selection(at[[yz ^ own for yz in range(4)]].transpose(4, 1, 2, 0, 3), 256)
            for own in range(4)
        ]
    )


FIRST, SECOND = phase_picks()
FINAL = final_picks()


def dot(a, b):
    return jnp.dot(a, b, preferred_element_type=F32)


def in_hbm(value):
    return pltpu.with_memory_space_constraint(value, pltpu.HBM)


def params(mebibytes):
    return pltpu.CompilerParams(vmem_limit_bytes=mebibytes * 1024 * 1024)


def rotate_kernel(place, *refs):
    blocks, angles = refs[0:4], refs[4:8]
    mix_ref, first, second, angle, mixed = refs[8:]
    for j in range(4):
        for x2 in range(2):
            for y in range(2):
                angle[j, x2, 4 * y : 4 * y + 4, :] = angles[j][0, x2, 0, y]
            sine, cosine = sin_cos(angle[j, x2])
            for low in range(8):
                block = blocks[j][x2, 0, 16 * low : 16 * low + 16, :].astype(F32)
                re, im = block[:8], block[8:]
                s, c = sine[low : low + 1], cosine[low : low + 1]
                turned = jnp.concatenate([re * c - im * s, re * s + im * c], axis=0)
                at = 128 * x2 + 16 * low
                mixed[j, at : at + 16, :] = turned.astype(BF)
        (first, second)[j // 2][j % 2] = dot(mix_ref[...], mixed[j]).astype(BF)


def rotate(place, weights, angles, keep):
    def block(j):
        y, z = ((1, 0), (1, 1), (0, 1), (1, 1))[j] if keep else ((0, 0), (0, 1), (0, 0), (1, 0))[j]
        return lambda p: (p[0] ^ (1 - y)) * 2 + (p[1] ^ (1 - z))

    def weight(j):
        at = block(j)
        return pl.BlockSpec((2, 1, 128, CHEB), lambda i, p: (0, at(p), j // 2, 0))

    def phase(j):
        at = block(j)
        return pl.BlockSpec((1, 2, 1, 2, 4, CHEB), lambda i, p: (0, 0, at(p), j // 2, 0, 0))

    spec = pltpu.PrefetchScalarGridSpec(
        num_scalar_prefetch=1,
        grid=(1,),
        in_specs=[weight(j) for j in range(4)]
        + [phase(j) for j in range(4)]
        + [pl.BlockSpec((256, 256), lambda i, p: (0, 0))],
        out_specs=[pl.BlockSpec((2, 256, CHEB), lambda i, p: (0, 0, 0))] * 2,
        scratch_shapes=[pltpu.VMEM((4, 2, 8, CHEB), F32), pltpu.VMEM((4, 256, CHEB), BF)],
    )
    return pl.pallas_call(
        rotate_kernel,
        grid_spec=spec,
        out_shape=[jax.ShapeDtypeStruct((2, 256, CHEB), BF)] * 2,
        compiler_params=params(12),
        name="rotate_kept" if keep else "rotate_sent",
    )(place, *[weights] * 4, *[angles] * 4, in_hbm(jnp.asarray(MIX, BF)))


def phase_kernel(a1_ref, a2_ref, order_ref, phases, far):
    for block in range(4):
        for level, ref in enumerate((a1_ref, a2_ref)):
            for x2 in range(2):
                for y in range(4):
                    at = 32 * level + 16 * x2 + 4 * y
                    far[block, at : at + 4, :] = ref[0, x2, block, y]
        value = far[block].astype(BF)
        value = jnp.concatenate([value[:, :HALF], value[:, HALF:]], axis=0)
        value = dot(order_ref[...], value).astype(BF)
        for high in range(2):
            phases[high, block] = value[64 * high : 64 * high + 64]


def far_phases(angles):
    return pl.pallas_call(
        phase_kernel,
        grid=(1,),
        in_specs=[
            pl.BlockSpec((1, 2, 4, 4, 4, CHEB), lambda i: (1, 0, 0, 0, 0, 0)),
            pl.BlockSpec((1, 2, 4, 4, 4, CHEB), lambda i: (2, 0, 0, 0, 0, 0)),
            pl.BlockSpec((128, 128), lambda i: (0, 0)),
        ],
        out_specs=pl.BlockSpec((2, 4, 64, HALF), lambda i: (0, 0, 0, 0)),
        out_shape=jax.ShapeDtypeStruct((2, 4, 64, HALF), BF),
        scratch_shapes=[pltpu.VMEM((4, 64, CHEB), F32)],
        compiler_params=params(8),
        name="far_phases",
    )(angles, angles, in_hbm(jnp.asarray(SEND_PHASE, BF)))


def add(a, b):
    return (a.astype(F32) + b.astype(F32)).astype(BF)


def sum_kernel(keep0, come0, again0, keep1, come1, again1, out_ref):
    for half, (kept, come, again) in enumerate(((keep0, come0, again0), (keep1, come1, again1))):
        out_ref[half] = add(add(kept[1], come[1]), again[...])


def sums(*args):
    return pl.pallas_call(
        sum_kernel,
        out_shape=jax.ShapeDtypeStruct((2, 256, CHEB), BF),
        in_specs=[pl.BlockSpec(memory_space=pltpu.VMEM)] * 6,
        out_specs=pl.BlockSpec(memory_space=pltpu.VMEM),
        compiler_params=params(8),
        name="sums",
    )(*args)


def trig_kernel(place, *refs):
    near1, near2 = refs[0:4], refs[4:8]
    first_ref, second_ref, out_ref = refs[8:]
    step = pl.program_id(0)

    def write(t, angle):
        for half in range(2):
            for at in range(0, 64, 8):
                sine, cosine = sin_cos(angle[64 * half + at : 64 * half + at + 8])
                out_ref[t, 0, at : at + 8, HALF * half : HALF * half + HALF] = sine
                out_ref[t, 1, at : at + 8, HALF * half : HALF * half + HALF] = cosine

    @pl.when(step < 2)
    def _():
        for t in range(4):
            held = jnp.concatenate([r[t] for r in near1], axis=0)
            write(t, dot(first_ref[0], held))

    @pl.when(step >= 2)
    def _():
        for t in range(4):
            held = [r[:, 8 * t : 8 * t + 8, :].astype(F32).reshape(64, HALF) for r in near2]
            write(t, dot(second_ref[0], jnp.concatenate(held, axis=0).astype(BF)))


def trig(place, near):
    def own(*shape):
        return pl.BlockSpec((1, *shape), lambda i, p: (p[2],) + (0,) * len(shape))

    spec = pltpu.PrefetchScalarGridSpec(
        num_scalar_prefetch=1,
        grid=(4,),
        in_specs=[pl.BlockSpec((4, 64, HALF), lambda i, p: (jnp.minimum(i, 1), 0, 0))] * 4
        + [pl.BlockSpec((8, 32, HALF), lambda i, p: (0, jnp.maximum(i - 2, 0), 0))] * 4
        + [own(128, 256), own(128, 256)],
        out_specs=pl.BlockSpec((4, 2, 64, CHEB), lambda i, p: (i, 0, 0, 0)),
    )
    return pl.pallas_call(
        trig_kernel,
        grid_spec=spec,
        out_shape=pltpu.HBM((16, 2, 64, CHEB), F32),
        compiler_params=params(12),
        name="trig",
    )(place, *near, *near, jnp.asarray(FIRST, BF), jnp.asarray(SECOND, BF))


def levels_kernel(x_ref, t_ref, trig_ref, enter_ref, turn_ref, leave_ref, out_ref, left, middle, even, odd):
    step = pl.program_id(0)

    @pl.when(step == 0)
    def _():
        total = (x_ref[0].astype(F32) + x_ref[1].astype(F32)).astype(BF)
        left[...] = dot(enter_ref[...], total).astype(BF)

    @pl.when(step == 2)
    def _():
        left[...] = dot(turn_ref[...], middle[...]).astype(BF)

    def turn_and_sum(product, at):
        total = [jnp.zeros((8, CHEB), F32)] * 4
        for outer in range(8):
            sine = trig_ref[at, 0, 8 * outer : 8 * outer + 8, :]
            cosine = trig_ref[at, 1, 8 * outer : 8 * outer + 8, :]
            for r in range(2):
                row = 32 * outer + 8 * r
                re = product[row : row + 8, :]
                im = product[row + 16 : row + 24, :]
                total[r] = total[r] + (re * cosine - im * sine)
                total[2 + r] = total[2 + r] + (re * sine + im * cosine)
        return jnp.concatenate(total, axis=0).astype(BF)

    def four_orientations(put):
        even[...] = dot(left[...], t_ref[0])
        for t in range(4):
            if t < 3:
                (odd, even)[t % 2][...] = dot(left[...], t_ref[t + 1])
            put(t, turn_and_sum((even, odd)[t % 2], t))

    @pl.when(step < 2)
    def _():
        def put(t, value):
            row = pl.multiple_of(128 * step + 32 * t, 32)
            middle[pl.ds(row, 32), :] = value

        four_orientations(put)

    @pl.when(step >= 2)
    def _():
        def put(t, value):
            value = jnp.concatenate([value[:, :HALF], value[:, HALF:]], axis=0)
            value = dot(leave_ref[...], value)
            for t4 in range(8):
                out_ref[t4, t] = value[8 * t4 : 8 * t4 + 8].astype(BF)

        four_orientations(put)


def levels(share, translation, waves):
    def const(*shape):
        return pl.BlockSpec(shape, lambda i: (0,) * len(shape))

    return pl.pallas_call(
        levels_kernel,
        grid=(4,),
        out_shape=jax.ShapeDtypeStruct((8, 8, 8, HALF), BF),
        in_specs=[
            const(2, 256, CHEB),
            pl.BlockSpec((4, CHEB, CHEB), lambda i: (i % 2, 0, 0)),
            pl.BlockSpec((4, 2, 64, CHEB), lambda i: (i, 0, 0, 0)),
            const(256, 256),
            const(256, 256),
            const(64, 64),
        ],
        out_specs=pl.BlockSpec((8, 4, 8, HALF), lambda i: (0, jnp.maximum(i - 2, 0), 0, 0)),
        scratch_shapes=[
            pltpu.VMEM((256, CHEB), BF),
            pltpu.VMEM((256, CHEB), BF),
            pltpu.VMEM((256, CHEB), F32),
            pltpu.VMEM((256, CHEB), F32),
        ],
        compiler_params=params(20),
        name="levels",
    )(share, in_hbm(translation), in_hbm(waves), jnp.asarray(ENTER, BF), jnp.asarray(TURN, BF), jnp.asarray(LEAVE, BF))


def final_kernel(place, n0, n1, n2, n3, pick_ref, t_ref, out_ref, left):
    for high in range(2):
        held = jnp.concatenate([r[64 * high : 64 * high + 64] for r in (n0, n1, n2, n3)], axis=0)
        value = dot(pick_ref[0], held)
        value = jnp.concatenate([value[:128], value[128:]], axis=1)
        left[128 * high : 128 * high + 128, :] = value.astype(BF)
    for x2 in range(2):
        out_ref[x2, 0] = dot(left[...], t_ref[4 * x2 + place[2]]).astype(BF)


def final(place, near, translation):
    spec = pltpu.PrefetchScalarGridSpec(
        num_scalar_prefetch=1,
        grid=(4,),
        in_specs=[pl.BlockSpec((128, HALF), lambda i, p: (i, 0))] * 4
        + [
            pl.BlockSpec((1, 256, 256), lambda i, p: (p[2], 0, 0)),
            pl.BlockSpec(memory_space=pltpu.VMEM),
        ],
        out_specs=pl.BlockSpec((2, 1, 256, CHEB), lambda i, p: (0, i, 0, 0)),
        scratch_shapes=[pltpu.VMEM((256, CHEB), BF)],
    )
    return pl.pallas_call(
        final_kernel,
        grid_spec=spec,
        out_shape=jax.ShapeDtypeStruct((2, 4, 256, CHEB), BF),
        compiler_params=params(14),
        name="final",
    )(place, *near, jnp.asarray(FINAL, BF), translation)


def swap(value, axis):
    return lax.ppermute(value, axis, [(0, 1), (1, 0)])


def four(value):
    other = swap(value, "y2")
    return value, swap(value, "z2"), other, swap(other, "z2")


def exchange(value, axes):
    return lax.all_to_all(value, axes, split_axis=0, concat_axis=0, tiled=True)


def shards(weights, angles, translation):
    bit = lax.axis_index
    place = jnp.stack([bit("y4"), bit("z4"), 2 * bit("y2") + bit("z2")]).astype(jnp.int32)
    shape = weights.shape
    weights = in_hbm(weights.reshape(2, 4, 256, CHEB))
    angles = in_hbm(angles.reshape(3, 2, 4, 4, 4, CHEB))
    send0, send1 = rotate(place, weights, angles, False)
    come0, come1 = swap(send0, "y4"), swap(send1, "z4")
    keep0, keep1 = rotate(place, weights, angles, True)
    phases = exchange(far_phases(angles).reshape(64, 8, HALF), ("x4", "y4", "z4", "x3", "y3", "z3"))
    again0, again1 = add(keep0[0], come0[0]), add(keep1[0], come1[0])
    phases, _, _ = lax.optimization_barrier((phases, again0, again1))
    near = four(phases.reshape(8, 64, HALF))
    again0, again1 = swap(again0, "z4"), swap(again1, "y4")
    share = sums(keep0, come0, again0, keep1, come1, again1)
    share, near = lax.optimization_barrier((share, near))
    share = exchange(share.reshape(64, 8, CHEB), ("x4", "x3", "y3", "z3", "y2", "z2"))
    waves = trig(place, near)
    done = levels(share.reshape(2, 256, CHEB), translation, waves)
    done = exchange(done.reshape(64, 8, HALF), ("y4", "z4", "x4", "x3", "y3", "z3"))
    near = four(done.reshape(512, HALF))
    return final(place, near, translation).reshape(shape)


def solution(mesh):
    fine = Mesh(mesh.devices.reshape((2,) * len(BITS)), BITS)
    x, y, z = BITS[:2], BITS[2:5], BITS[5:]
    return jax.shard_map(
        shards,
        mesh=fine,
        in_specs=(P(x, y, z, None, None, None), P(None, x, y, z, None), P()),
        out_specs=P(x, y, z, None, None, None),
        check_vma=False,
    )
```

```python
import jax
import jax.numpy as jnp
import numpy as np
from jax import lax
from jax.experimental import pallas as pl
from jax.experimental.pallas import tpu as pltpu
from jax.sharding import Mesh
from jax.sharding import PartitionSpec as P

BITS = ("x4", "x3", "y4", "y3", "y2", "z4", "z3", "z2")
CHEB = 512
HALF = 256
BF = jnp.bfloat16
F32 = jnp.float32

SIN = (1.0, -0.1666666567325592, 0.00833332072943449, -0.00019840527966152877, 2.753572516667191e-06,
       -2.472758353633253e-08, 1.3608578153245787e-10)
COS = (1.0, -0.49999988079071045, 0.04166648909449577, -0.0013887794921174645, 2.4769700758042745e-05,
       -2.707722615014063e-07, 1.7238451777146224e-09)


def sin_cos(angle):
    square = angle * angle
    sine, cosine = jnp.full_like(square, SIN[-1]), jnp.full_like(square, COS[-1])
    for s, c in zip(SIN[-2::-1], COS[-2::-1]):
        sine, cosine = sine * square + s, cosine * square + c
    return sine * angle, cosine


def selection(source, count):
    source = np.asarray(source).reshape(-1)
    matrix = np.zeros((source.size, count), np.float32)
    matrix[np.arange(source.size), source] = 1
    return matrix


def rows(dims, order):
    return np.arange(int(np.prod(dims))).reshape(dims).transpose(order)


MIX = selection(rows((2, 8, 2, 4, 2), (1, 3, 0, 2, 4)), 256)
SEND_PHASE = selection(rows((2, 2, 2, 16), (3, 1, 2, 0)), 128)
ENTER = selection(rows((8, 4, 2, 2, 2), (0, 3, 4, 1, 2)), 256)
TURN = selection(rows((8, 2, 2, 8), (3, 1, 2, 0)), 256)
LEAVE = selection(rows((2, 2, 2, 2, 2, 2), (4, 5, 3, 1, 2, 0)), 64)


def phase_picks():
    first, second = [], []
    at = np.arange(256).reshape(4, 8, 2, 2, 2)
    for own in range(4):
        near = at[[yz ^ own for yz in range(4)]]
        first.append(selection(near[:, :, 0].transpose(3, 1, 0, 2), 256))
        second.append(selection(near[:, :, 1].transpose(3, 0, 2, 1), 256))
    return np.stack(first), np.stack(second)


def final_picks():
    at = np.arange(256).reshape(4, 8, 2, 2, 2)
    return np.stack(
        [
            selection(at[[yz ^ own for yz in range(4)]].transpose(4, 1, 2, 0, 3), 256)
            for own in range(4)
        ]
    )


FIRST, SECOND = phase_picks()
FINAL = final_picks()


def dot(a, b):
    return jnp.dot(a, b, preferred_element_type=F32)


def in_hbm(value):
    return pltpu.with_memory_space_constraint(value, pltpu.HBM)


def params(mebibytes):
    return pltpu.CompilerParams(vmem_limit_bytes=mebibytes * 1024 * 1024)


def rotate_kernel(place, *refs):
    blocks, angles = refs[0:4], refs[4:8]
    mix_ref, first, second, angle, mixed = refs[8:]
    for j in range(4):
        for x2 in range(2):
            for y in range(2):
                angle[j, x2, 4 * y : 4 * y + 4, :] = angles[j][0, x2, 0, y]
            sine, cosine = sin_cos(angle[j, x2])
            for low in range(8):
                block = blocks[j][x2, 0, 16 * low : 16 * low + 16, :].astype(F32)
                re, im = block[:8], block[8:]
                s, c = sine[low : low + 1], cosine[low : low + 1]
                turned = jnp.concatenate([re * c - im * s, re * s + im * c], axis=0)
                at = 128 * x2 + 16 * low
                mixed[j, at : at + 16, :] = turned.astype(BF)
        (first, second)[j // 2][j % 2] = dot(mix_ref[...], mixed[j]).astype(BF)


def rotate(place, weights, angles, keep):
    def block(j):
        y, z = ((1, 0), (1, 1), (0, 1), (1, 1))[j] if keep else ((0, 0), (0, 1), (0, 0), (1, 0))[j]
        return lambda p: (p[0] ^ (1 - y)) * 2 + (p[1] ^ (1 - z))

    def weight(j):
        at = block(j)
        return pl.BlockSpec((2, 1, 128, CHEB), lambda i, p: (0, at(p), j // 2, 0))

    def phase(j):
        at = block(j)
        return pl.BlockSpec((1, 2, 1, 2, 4, CHEB), lambda i, p: (0, 0, at(p), j // 2, 0, 0))

    spec = pltpu.PrefetchScalarGridSpec(
        num_scalar_prefetch=1,
        grid=(1,),
        in_specs=[weight(j) for j in range(4)]
        + [phase(j) for j in range(4)]
        + [pl.BlockSpec((256, 256), lambda i, p: (0, 0))],
        out_specs=[pl.BlockSpec((2, 256, CHEB), lambda i, p: (0, 0, 0))] * 2,
        scratch_shapes=[pltpu.VMEM((4, 2, 8, CHEB), F32), pltpu.VMEM((4, 256, CHEB), BF)],
    )
    return pl.pallas_call(
        rotate_kernel,
        grid_spec=spec,
        out_shape=[jax.ShapeDtypeStruct((2, 256, CHEB), BF)] * 2,
        compiler_params=params(12),
        name="rotate_kept" if keep else "rotate_sent",
    )(place, *[weights] * 4, *[angles] * 4, in_hbm(jnp.asarray(MIX, BF)))


def phase_kernel(a1_ref, a2_ref, order_ref, phases, far):
    for block in range(4):
        for level, ref in enumerate((a1_ref, a2_ref)):
            for x2 in range(2):
                for y in range(4):
                    at = 32 * level + 16 * x2 + 4 * y
                    far[block, at : at + 4, :] = ref[0, x2, block, y]
        value = far[block].astype(BF)
        value = jnp.concatenate([value[:, :HALF], value[:, HALF:]], axis=0)
        value = dot(order_ref[...], value).astype(BF)
        for high in range(2):
            phases[high, block] = value[64 * high : 64 * high + 64]


def far_phases(angles):
    return pl.pallas_call(
        phase_kernel,
        grid=(1,),
        in_specs=[
            pl.BlockSpec((1, 2, 4, 4, 4, CHEB), lambda i: (1, 0, 0, 0, 0, 0)),
            pl.BlockSpec((1, 2, 4, 4, 4, CHEB), lambda i: (2, 0, 0, 0, 0, 0)),
            pl.BlockSpec((128, 128), lambda i: (0, 0)),
        ],
        out_specs=pl.BlockSpec((2, 4, 64, HALF), lambda i: (0, 0, 0, 0)),
        out_shape=jax.ShapeDtypeStruct((2, 4, 64, HALF), BF),
        scratch_shapes=[pltpu.VMEM((4, 64, CHEB), F32)],
        compiler_params=params(8),
        name="far_phases",
    )(angles, angles, in_hbm(jnp.asarray(SEND_PHASE, BF)))


def add(a, b):
    return (a.astype(F32) + b.astype(F32)).astype(BF)


def sum_kernel(keep0, come0, again0, keep1, come1, again1, out_ref):
    for half, (kept, come, again) in enumerate(((keep0, come0, again0), (keep1, come1, again1))):
        out_ref[half] = add(add(kept[1], come[1]), again[...])


def sums(*args):
    return pl.pallas_call(
        sum_kernel,
        out_shape=jax.ShapeDtypeStruct((2, 256, CHEB), BF),
        in_specs=[pl.BlockSpec(memory_space=pltpu.VMEM)] * 6,
        out_specs=pl.BlockSpec(memory_space=pltpu.VMEM),
        compiler_params=params(8),
        name="sums",
    )(*args)


def trig_kernel(place, *refs):
    near1, near2 = refs[0:4], refs[4:8]
    first_ref, second_ref, out_ref = refs[8:]
    step = pl.program_id(0)

    def write(t, angle):
        for half in range(2):
            for at in range(0, 64, 8):
                sine, cosine = sin_cos(angle[64 * half + at : 64 * half + at + 8])
                out_ref[t, 0, at : at + 8, HALF * half : HALF * half + HALF] = sine
                out_ref[t, 1, at : at + 8, HALF * half : HALF * half + HALF] = cosine

    @pl.when(step < 2)
    def _():
        for t in range(4):
            held = jnp.concatenate([r[t] for r in near1], axis=0)
            write(t, dot(first_ref[0], held))

    @pl.when(step >= 2)
    def _():
        for t in range(4):
            held = [r[:, 8 * t : 8 * t + 8, :].astype(F32).reshape(64, HALF) for r in near2]
            write(t, dot(second_ref[0], jnp.concatenate(held, axis=0).astype(BF)))


def trig(place, near):
    def own(*shape):
        return pl.BlockSpec((1, *shape), lambda i, p: (p[2],) + (0,) * len(shape))

    spec = pltpu.PrefetchScalarGridSpec(
        num_scalar_prefetch=1,
        grid=(4,),
        in_specs=[pl.BlockSpec((4, 64, HALF), lambda i, p: (jnp.minimum(i, 1), 0, 0))] * 4
        + [pl.BlockSpec((8, 32, HALF), lambda i, p: (0, jnp.maximum(i - 2, 0), 0))] * 4
        + [own(128, 256), own(128, 256)],
        out_specs=pl.BlockSpec((4, 2, 64, CHEB), lambda i, p: (i, 0, 0, 0)),
    )
    return pl.pallas_call(
        trig_kernel,
        grid_spec=spec,
        out_shape=pltpu.HBM((16, 2, 64, CHEB), F32),
        compiler_params=params(12),
        cost_estimate=pl.CostEstimate(flops=7 * 10**9, bytes_accessed=10**6, transcendentals=0),
        name="trig",
    )(place, *near, *near, in_hbm(jnp.asarray(FIRST, BF)), in_hbm(jnp.asarray(SECOND, BF)))


def levels_kernel(x_ref, t_ref, trig_ref, enter_ref, turn_ref, leave_ref, out_ref, left, middle, even, odd):
    step = pl.program_id(0)

    @pl.when(step == 0)
    def _():
        total = (x_ref[0].astype(F32) + x_ref[1].astype(F32)).astype(BF)
        left[...] = dot(enter_ref[...], total).astype(BF)

    @pl.when(step == 2)
    def _():
        left[...] = dot(turn_ref[...], middle[...]).astype(BF)

    def turn_and_sum(product, at):
        total = [jnp.zeros((8, CHEB), F32)] * 4
        for outer in range(8):
            sine = trig_ref[at, 0, 8 * outer : 8 * outer + 8, :]
            cosine = trig_ref[at, 1, 8 * outer : 8 * outer + 8, :]
            for r in range(2):
                row = 32 * outer + 8 * r
                re = product[row : row + 8, :]
                im = product[row + 16 : row + 24, :]
                total[r] = total[r] + (re * cosine - im * sine)
                total[2 + r] = total[2 + r] + (re * sine + im * cosine)
        return jnp.concatenate(total, axis=0).astype(BF)

    def four_orientations(put):
        even[...] = dot(left[...], t_ref[0])
        for t in range(4):
            if t < 3:
                (odd, even)[t % 2][...] = dot(left[...], t_ref[t + 1])
            put(t, turn_and_sum((even, odd)[t % 2], t))

    @pl.when(step < 2)
    def _():
        def put(t, value):
            row = pl.multiple_of(128 * step + 32 * t, 32)
            middle[pl.ds(row, 32), :] = value

        four_orientations(put)

    @pl.when(step >= 2)
    def _():
        def put(t, value):
            value = jnp.concatenate([value[:, :HALF], value[:, HALF:]], axis=0)
            value = dot(leave_ref[...], value)
            for t4 in range(8):
                out_ref[t4, t] = value[8 * t4 : 8 * t4 + 8].astype(BF)

        four_orientations(put)


def levels(share, translation, waves):
    def const(*shape):
        return pl.BlockSpec(shape, lambda i: (0,) * len(shape))

    return pl.pallas_call(
        levels_kernel,
        grid=(4,),
        out_shape=jax.ShapeDtypeStruct((8, 8, 8, HALF), BF),
        in_specs=[
            const(2, 256, CHEB),
            pl.BlockSpec((4, CHEB, CHEB), lambda i: (i % 2, 0, 0)),
            pl.BlockSpec((4, 2, 64, CHEB), lambda i: (i, 0, 0, 0)),
            const(256, 256),
            const(256, 256),
            const(64, 64),
        ],
        out_specs=pl.BlockSpec((8, 4, 8, HALF), lambda i: (0, jnp.maximum(i - 2, 0), 0, 0)),
        scratch_shapes=[
            pltpu.VMEM((256, CHEB), BF),
            pltpu.VMEM((256, CHEB), BF),
            pltpu.VMEM((256, CHEB), F32),
            pltpu.VMEM((256, CHEB), F32),
        ],
        compiler_params=params(20),
        name="levels",
    )(share, in_hbm(translation), in_hbm(waves), jnp.asarray(ENTER, BF), jnp.asarray(TURN, BF), jnp.asarray(LEAVE, BF))


def final_kernel(place, n0, n1, n2, n3, pick_ref, t_ref, out_ref, left):
    for high in range(2):
        held = jnp.concatenate([r[64 * high : 64 * high + 64] for r in (n0, n1, n2, n3)], axis=0)
        value = dot(pick_ref[0], held)
        value = jnp.concatenate([value[:128], value[128:]], axis=1)
        left[128 * high : 128 * high + 128, :] = value.astype(BF)
    for x2 in range(2):
        out_ref[x2, 0] = dot(left[...], t_ref[4 * x2 + place[2]]).astype(BF)


def final(place, near, translation):
    spec = pltpu.PrefetchScalarGridSpec(
        num_scalar_prefetch=1,
        grid=(4,),
        in_specs=[pl.BlockSpec((128, HALF), lambda i, p: (i, 0))] * 4
        + [
            pl.BlockSpec((1, 256, 256), lambda i, p: (p[2], 0, 0)),
            pl.BlockSpec(memory_space=pltpu.VMEM),
        ],
        out_specs=pl.BlockSpec((2, 1, 256, CHEB), lambda i, p: (0, i, 0, 0)),
        scratch_shapes=[pltpu.VMEM((256, CHEB), BF)],
    )
    return pl.pallas_call(
        final_kernel,
        grid_spec=spec,
        out_shape=jax.ShapeDtypeStruct((2, 4, 256, CHEB), BF),
        compiler_params=params(14),
        name="final",
    )(place, *near, jnp.asarray(FINAL, BF), translation)


def swap(value, axis):
    return lax.ppermute(value, axis, [(0, 1), (1, 0)])


def four(value):
    other = swap(value, "y2")
    return value, swap(value, "z2"), other, swap(other, "z2")


def exchange(value, axes):
    return lax.all_to_all(value, axes, split_axis=0, concat_axis=0, tiled=True)


def shards(weights, angles, translation):
    bit = lax.axis_index
    place = jnp.stack([bit("y4"), bit("z4"), 2 * bit("y2") + bit("z2")]).astype(jnp.int32)
    shape = weights.shape
    weights = in_hbm(weights.reshape(2, 4, 256, CHEB))
    angles = in_hbm(angles.reshape(3, 2, 4, 4, 4, CHEB))
    send0, send1 = rotate(place, weights, angles, False)
    come0, come1 = swap(send0, "y4"), swap(send1, "z4")
    keep0, keep1 = rotate(place, weights, angles, True)
    phases = exchange(far_phases(angles).reshape(64, 8, HALF), ("x4", "y4", "z4", "x3", "y3", "z3"))
    again0, again1 = add(keep0[0], come0[0]), add(keep1[0], come1[0])
    phases, _, _ = lax.optimization_barrier((phases, again0, again1))
    near = four(phases.reshape(8, 64, HALF))
    again0, again1 = swap(again0, "z4"), swap(again1, "y4")
    share = sums(keep0, come0, again0, keep1, come1, again1)
    share = exchange(share.reshape(64, 8, CHEB), ("x4", "x3", "y3", "z3", "y2", "z2"))
    waves = trig(place, near)
    done = levels(share.reshape(2, 256, CHEB), translation, waves)
    done = exchange(done.reshape(64, 8, HALF), ("y4", "z4", "x4", "x3", "y3", "z3"))
    near = four(done.reshape(512, HALF))
    return final(place, near, translation).reshape(shape)


def solution(mesh):
    fine = Mesh(mesh.devices.reshape((2,) * len(BITS)), BITS)
    x, y, z = BITS[:2], BITS[2:5], BITS[5:]
    return jax.shard_map(
        shards,
        mesh=fine,
        in_specs=(P(x, y, z, None, None, None), P(None, x, y, z, None), P()),
        out_specs=P(x, y, z, None, None, None),
        check_vma=False,
    )
```

```python
import jax
import jax.numpy as jnp
import numpy as np
from jax import lax
from jax.experimental import pallas as pl
from jax.experimental.pallas import tpu as pltpu
from jax.sharding import Mesh
from jax.sharding import PartitionSpec as P

BITS = ("x4", "x3", "y4", "y3", "y2", "z4", "z3", "z2")
CHEB = 512
HALF = 256
BF = jnp.bfloat16
F32 = jnp.float32

SIN = (1.0, -0.1666666567325592, 0.00833332072943449, -0.00019840527966152877, 2.753572516667191e-06,
       -2.472758353633253e-08, 1.3608578153245787e-10)
COS = (1.0, -0.49999988079071045, 0.04166648909449577, -0.0013887794921174645, 2.4769700758042745e-05,
       -2.707722615014063e-07, 1.7238451777146224e-09)


def sin_cos(angle):
    square = angle * angle
    sine, cosine = jnp.full_like(square, SIN[-1]), jnp.full_like(square, COS[-1])
    for s, c in zip(SIN[-2::-1], COS[-2::-1]):
        sine, cosine = sine * square + s, cosine * square + c
    return sine * angle, cosine


def selection(source, count):
    source = np.asarray(source).reshape(-1)
    matrix = np.zeros((source.size, count), np.float32)
    matrix[np.arange(source.size), source] = 1
    return matrix


def rows(dims, order):
    return np.arange(int(np.prod(dims))).reshape(dims).transpose(order)


MIX = selection(rows((2, 8, 2, 4, 2), (1, 3, 0, 2, 4)), 256)
SEND_PHASE = selection(rows((2, 2, 2, 16), (3, 1, 2, 0)), 128)
ENTER = selection(rows((8, 4, 2, 2, 2), (0, 3, 4, 1, 2)), 256)
TURN = selection(rows((8, 2, 2, 8), (3, 1, 2, 0)), 256)
LEAVE = selection(rows((2, 2, 2, 2, 2, 2), (4, 5, 3, 1, 2, 0)), 64)


def phase_picks():
    first, second = [], []
    at = np.arange(256).reshape(4, 8, 2, 2, 2)
    for own in range(4):
        near = at[[yz ^ own for yz in range(4)]]
        first.append(selection(near[:, :, 0].transpose(3, 1, 0, 2), 256))
        second.append(selection(near[:, :, 1].transpose(3, 0, 2, 1), 256))
    return np.stack(first), np.stack(second)


def final_picks():
    at = np.arange(256).reshape(4, 8, 2, 2, 2)
    return np.stack(
        [
            selection(at[[yz ^ own for yz in range(4)]].transpose(4, 1, 2, 0, 3), 256)
            for own in range(4)
        ]
    )


FIRST, SECOND = phase_picks()
FINAL = final_picks()


def dot(a, b):
    return jnp.dot(a, b, preferred_element_type=F32)


def in_hbm(value):
    return pltpu.with_memory_space_constraint(value, pltpu.HBM)


def params(mebibytes):
    return pltpu.CompilerParams(vmem_limit_bytes=mebibytes * 1024 * 1024)


def rotate_blocks(blocks, angles, mix_ref, first, second, angle, mixed):
    for j in range(4):
        for x2 in range(2):
            for y in range(2):
                angle[j, x2, 4 * y : 4 * y + 4, :] = angles[j][0, x2, 0, y]
            sine, cosine = sin_cos(angle[j, x2])
            for low in range(8):
                block = blocks[j][x2, 0, 16 * low : 16 * low + 16, :].astype(F32)
                re, im = block[:8], block[8:]
                s, c = sine[low : low + 1], cosine[low : low + 1]
                turned = jnp.concatenate([re * c - im * s, re * s + im * c], axis=0)
                at = 128 * x2 + 16 * low
                mixed[j, at : at + 16, :] = turned.astype(BF)
        (first, second)[j // 2][j % 2] = dot(mix_ref[...], mixed[j]).astype(BF)


def send_kernel(place, *refs):
    rotate_blocks(refs[0:4], refs[4:8], *refs[8:])


def keep_kernel(place, *refs):
    mix_ref, a1_ref, a2_ref, order_ref, first, second, phases, angle, mixed, far = refs[8:]
    for block in range(4):
        for level, ref in enumerate((a1_ref, a2_ref)):
            for x2 in range(2):
                for y in range(4):
                    at = 32 * level + 16 * x2 + 4 * y
                    far[block, at : at + 4, :] = ref[0, x2, block, y]
        value = far[block].astype(BF)
        value = jnp.concatenate([value[:, :HALF], value[:, HALF:]], axis=0)
        value = dot(order_ref[...], value).astype(BF)
        for high in range(2):
            phases[high, block] = value[64 * high : 64 * high + 64]
    rotate_blocks(refs[0:4], refs[4:8], mix_ref, first, second, angle, mixed)


def rotate(place, weights, angles, keep):
    def block(j):
        y, z = ((1, 0), (1, 1), (0, 1), (1, 1))[j] if keep else ((0, 0), (0, 1), (0, 0), (1, 0))[j]
        return lambda p: (p[0] ^ (1 - y)) * 2 + (p[1] ^ (1 - z))

    def weight(j):
        at = block(j)
        return pl.BlockSpec((2, 1, 128, CHEB), lambda i, p: (0, at(p), j // 2, 0))

    def phase(j):
        at = block(j)
        return pl.BlockSpec((1, 2, 1, 2, 4, CHEB), lambda i, p: (0, 0, at(p), j // 2, 0, 0))

    in_specs = [weight(j) for j in range(4)] + [phase(j) for j in range(4)]
    in_specs.append(pl.BlockSpec((256, 256), lambda i, p: (0, 0)))
    out_specs = [pl.BlockSpec((2, 256, CHEB), lambda i, p: (0, 0, 0))] * 2
    out_shape = [jax.ShapeDtypeStruct((2, 256, CHEB), BF)] * 2
    scratch = [pltpu.VMEM((4, 2, 8, CHEB), F32), pltpu.VMEM((4, 256, CHEB), BF)]
    args = [*[weights] * 4, *[angles] * 4, in_hbm(jnp.asarray(MIX, BF))]
    if keep:
        in_specs += [
            pl.BlockSpec((1, 2, 4, 4, 4, CHEB), lambda i, p: (1, 0, 0, 0, 0, 0)),
            pl.BlockSpec((1, 2, 4, 4, 4, CHEB), lambda i, p: (2, 0, 0, 0, 0, 0)),
            pl.BlockSpec((128, 128), lambda i, p: (0, 0)),
        ]
        out_specs.append(pl.BlockSpec((2, 4, 64, HALF), lambda i, p: (0, 0, 0, 0)))
        out_shape.append(jax.ShapeDtypeStruct((2, 4, 64, HALF), BF))
        scratch.append(pltpu.VMEM((4, 64, CHEB), F32))
        args += [angles, angles, in_hbm(jnp.asarray(SEND_PHASE, BF))]
    spec = pltpu.PrefetchScalarGridSpec(
        num_scalar_prefetch=1, grid=(1,), in_specs=in_specs, out_specs=out_specs, scratch_shapes=scratch
    )
    return pl.pallas_call(
        keep_kernel if keep else send_kernel,
        grid_spec=spec,
        out_shape=out_shape,
        compiler_params=params(14),
        name="rotate_kept" if keep else "rotate_sent",
    )(place, *args)


def add(a, b):
    return (a.astype(F32) + b.astype(F32)).astype(BF)


def sum_kernel(keep0, come0, again0, keep1, come1, again1, out_ref):
    for half, (kept, come, again) in enumerate(((keep0, come0, again0), (keep1, come1, again1))):
        out_ref[half] = add(add(kept[1], come[1]), again[...])


def sums(*args):
    return pl.pallas_call(
        sum_kernel,
        out_shape=jax.ShapeDtypeStruct((2, 256, CHEB), BF),
        in_specs=[pl.BlockSpec(memory_space=pltpu.VMEM)] * 6,
        out_specs=pl.BlockSpec(memory_space=pltpu.VMEM),
        compiler_params=params(8),
        name="sums",
    )(*args)


def trig_kernel(place, *refs):
    near1, near2 = refs[0:4], refs[4:8]
    first_ref, second_ref, out_ref = refs[8:]
    step = pl.program_id(0)

    def write(t, angle):
        for half in range(2):
            for at in range(0, 64, 8):
                sine, cosine = sin_cos(angle[64 * half + at : 64 * half + at + 8])
                out_ref[t, 0, at : at + 8, HALF * half : HALF * half + HALF] = sine
                out_ref[t, 1, at : at + 8, HALF * half : HALF * half + HALF] = cosine

    @pl.when(step < 2)
    def _():
        for t in range(4):
            held = jnp.concatenate([r[t] for r in near1], axis=0)
            write(t, dot(first_ref[0], held))

    @pl.when(step >= 2)
    def _():
        for t in range(4):
            held = [r[:, 8 * t : 8 * t + 8, :].astype(F32).reshape(64, HALF) for r in near2]
            write(t, dot(second_ref[0], jnp.concatenate(held, axis=0).astype(BF)))


def trig(place, near):
    def own(*shape):
        return pl.BlockSpec((1, *shape), lambda i, p: (p[2],) + (0,) * len(shape))

    spec = pltpu.PrefetchScalarGridSpec(
        num_scalar_prefetch=1,
        grid=(4,),
        in_specs=[pl.BlockSpec((4, 64, HALF), lambda i, p: (jnp.minimum(i, 1), 0, 0))] * 4
        + [pl.BlockSpec((8, 32, HALF), lambda i, p: (0, jnp.maximum(i - 2, 0), 0))] * 4
        + [own(128, 256), own(128, 256)],
        out_specs=pl.BlockSpec((4, 2, 64, CHEB), lambda i, p: (i, 0, 0, 0)),
    )
    return pl.pallas_call(
        trig_kernel,
        grid_spec=spec,
        out_shape=pltpu.HBM((16, 2, 64, CHEB), F32),
        compiler_params=params(12),
        cost_estimate=pl.CostEstimate(flops=7 * 10**9, bytes_accessed=10**6, transcendentals=0),
        name="trig",
    )(place, *near, *near, in_hbm(jnp.asarray(FIRST, BF)), in_hbm(jnp.asarray(SECOND, BF)))


def levels_kernel(x_ref, t_ref, trig_ref, enter_ref, turn_ref, leave_ref, out_ref, left, middle, even, odd):
    step = pl.program_id(0)

    @pl.when(step == 0)
    def _():
        total = (x_ref[0].astype(F32) + x_ref[1].astype(F32)).astype(BF)
        left[...] = dot(enter_ref[...], total).astype(BF)

    @pl.when(step == 2)
    def _():
        left[...] = dot(turn_ref[...], middle[...]).astype(BF)

    def turn_and_sum(product, at):
        total = [jnp.zeros((8, CHEB), F32)] * 4
        for outer in range(8):
            sine = trig_ref[at, 0, 8 * outer : 8 * outer + 8, :]
            cosine = trig_ref[at, 1, 8 * outer : 8 * outer + 8, :]
            for r in range(2):
                row = 32 * outer + 8 * r
                re = product[row : row + 8, :]
                im = product[row + 16 : row + 24, :]
                total[r] = total[r] + (re * cosine - im * sine)
                total[2 + r] = total[2 + r] + (re * sine + im * cosine)
        return jnp.concatenate(total, axis=0).astype(BF)

    def four_orientations(put):
        even[...] = dot(left[...], t_ref[0])
        for t in range(4):
            if t < 3:
                (odd, even)[t % 2][...] = dot(left[...], t_ref[t + 1])
            put(t, turn_and_sum((even, odd)[t % 2], t))

    @pl.when(step < 2)
    def _():
        def put(t, value):
            row = pl.multiple_of(128 * step + 32 * t, 32)
            middle[pl.ds(row, 32), :] = value

        four_orientations(put)

    @pl.when(step >= 2)
    def _():
        def put(t, value):
            value = jnp.concatenate([value[:, :HALF], value[:, HALF:]], axis=0)
            value = dot(leave_ref[...], value)
            for t4 in range(8):
                out_ref[t4, t] = value[8 * t4 : 8 * t4 + 8].astype(BF)

        four_orientations(put)


def levels(share, translation, waves):
    def const(*shape):
        return pl.BlockSpec(shape, lambda i: (0,) * len(shape))

    return pl.pallas_call(
        levels_kernel,
        grid=(4,),
        out_shape=jax.ShapeDtypeStruct((8, 8, 8, HALF), BF),
        in_specs=[
            const(2, 256, CHEB),
            pl.BlockSpec((4, CHEB, CHEB), lambda i: (i % 2, 0, 0)),
            pl.BlockSpec((4, 2, 64, CHEB), lambda i: (i, 0, 0, 0)),
            const(256, 256),
            const(256, 256),
            const(64, 64),
        ],
        out_specs=pl.BlockSpec((8, 4, 8, HALF), lambda i: (0, jnp.maximum(i - 2, 0), 0, 0)),
        scratch_shapes=[
            pltpu.VMEM((256, CHEB), BF),
            pltpu.VMEM((256, CHEB), BF),
            pltpu.VMEM((256, CHEB), F32),
            pltpu.VMEM((256, CHEB), F32),
        ],
        compiler_params=params(20),
        name="levels",
    )(share, in_hbm(translation), in_hbm(waves), jnp.asarray(ENTER, BF), jnp.asarray(TURN, BF), jnp.asarray(LEAVE, BF))


def final_kernel(place, n0, n1, n2, n3, pick_ref, t_ref, out_ref, left, made, sems):
    own = place[2]
    copies = []
    for block in range(4):
        for high in range(2):
            at = 128 * block + 64 * high
            held = jnp.concatenate([r[at : at + 64] for r in (n0, n1, n2, n3)], axis=0)
            value = dot(pick_ref[own], held)
            value = jnp.concatenate([value[:128], value[128:]], axis=1)
            left[block, 128 * high : 128 * high + 128, :] = value.astype(BF)
        for x2 in range(2):
            made[x2, block] = dot(left[block], t_ref[4 * x2 + own]).astype(BF)
            copies.append(
                pltpu.make_async_copy(made.at[x2, block], out_ref.at[x2, block], sems.at[x2, block])
            )
            copies[-1].start()
    for copy in copies:
        copy.wait()


def final(place, near, translation):
    vmem = pl.BlockSpec(memory_space=pltpu.VMEM)
    return pl.pallas_call(
        final_kernel,
        out_shape=jax.ShapeDtypeStruct((2, 4, 256, CHEB), BF),
        in_specs=[pl.BlockSpec(memory_space=pltpu.SMEM)] + [vmem] * 6,
        out_specs=pl.BlockSpec(memory_space=pl.ANY),
        scratch_shapes=[
            pltpu.VMEM((4, 256, CHEB), BF),
            pltpu.VMEM((2, 4, 256, CHEB), BF),
            pltpu.SemaphoreType.DMA((2, 4)),
        ],
        compiler_params=params(14),
        name="final",
    )(place, *near, jnp.asarray(FINAL, BF), translation)


def swap(value, axis):
    return lax.ppermute(value, axis, [(0, 1), (1, 0)])


def four(value):
    other = swap(value, "y2")
    return value, swap(value, "z2"), other, swap(other, "z2")


def exchange(value, axes):
    return lax.all_to_all(value, axes, split_axis=0, concat_axis=0, tiled=True)


def shards(weights, angles, translation):
    bit = lax.axis_index
    place = jnp.stack([bit("y4"), bit("z4"), 2 * bit("y2") + bit("z2")]).astype(jnp.int32)
    shape = weights.shape
    weights = in_hbm(weights.reshape(2, 4, 256, CHEB))
    angles = in_hbm(angles.reshape(3, 2, 4, 4, 4, CHEB))
    send0, send1 = rotate(place, weights, angles, False)
    come0, come1 = swap(send0, "y4"), swap(send1, "z4")
    keep0, keep1, phases = rotate(place, weights, angles, True)
    phases = exchange(phases.reshape(64, 8, HALF), ("x4", "y4", "z4", "x3", "y3", "z3"))
    again0, again1 = add(keep0[0], come0[0]), add(keep1[0], come1[0])
    phases, _, _ = lax.optimization_barrier((phases, again0, again1))
    near = four(phases.reshape(8, 64, HALF))
    again0, again1 = swap(again0, "z4"), swap(again1, "y4")
    share = sums(keep0, come0, again0, keep1, come1, again1)
    share = exchange(share.reshape(64, 8, CHEB), ("x4", "x3", "y3", "z3", "y2", "z2"))
    waves = trig(place, near)
    done = levels(share.reshape(2, 256, CHEB), translation, waves)
    done = exchange(done.reshape(64, 8, HALF), ("y4", "z4", "x4", "x3", "y3", "z3"))
    near = four(done.reshape(512, HALF))
    return final(place, near, translation).reshape(shape)


def solution(mesh):
    fine = Mesh(mesh.devices.reshape((2,) * len(BITS)), BITS)
    x, y, z = BITS[:2], BITS[2:5], BITS[5:]
    return jax.shard_map(
        shards,
        mesh=fine,
        in_specs=(P(x, y, z, None, None, None), P(None, x, y, z, None), P()),
        out_specs=P(x, y, z, None, None, None),
        check_vma=False,
    )
```

```python
import jax
import jax.numpy as jnp
import numpy as np
from jax import lax
from jax.experimental import pallas as pl
from jax.experimental.pallas import tpu as pltpu
from jax.sharding import Mesh
from jax.sharding import PartitionSpec as P

BITS = ("x4", "x3", "y4", "y3", "y2", "z4", "z3", "z2")
CHEB = 512
HALF = 256
BF = jnp.bfloat16
F32 = jnp.float32

SIN = (1.0, -0.1666666567325592, 0.00833332072943449, -0.00019840527966152877, 2.753572516667191e-06,
       -2.472758353633253e-08, 1.3608578153245787e-10)
COS = (1.0, -0.49999988079071045, 0.04166648909449577, -0.0013887794921174645, 2.4769700758042745e-05,
       -2.707722615014063e-07, 1.7238451777146224e-09)


def sin_cos(angle):
    square = angle * angle
    sine, cosine = jnp.full_like(square, SIN[-1]), jnp.full_like(square, COS[-1])
    for s, c in zip(SIN[-2::-1], COS[-2::-1]):
        sine, cosine = sine * square + s, cosine * square + c
    return sine * angle, cosine


def selection(source, count):
    source = np.asarray(source).reshape(-1)
    matrix = np.zeros((source.size, count), np.float32)
    matrix[np.arange(source.size), source] = 1
    return matrix


def rows(dims, order):
    return np.arange(int(np.prod(dims))).reshape(dims).transpose(order)


MIX = selection(rows((2, 8, 2, 4, 2), (1, 3, 0, 2, 4)), 256)
SEND_PHASE = selection(rows((2, 2, 2, 16), (3, 1, 2, 0)), 128)
ENTER = selection(rows((8, 4, 2, 2, 2), (0, 3, 4, 1, 2)), 256)
TURN = selection(rows((8, 2, 2, 8), (3, 1, 2, 0)), 256)
LEAVE = selection(rows((2, 2, 2, 2, 2, 2), (4, 5, 3, 1, 2, 0)), 64)


def phase_picks():
    first, second = [], []
    at = np.arange(256).reshape(4, 8, 2, 2, 2)
    for own in range(4):
        near = at[[yz ^ own for yz in range(4)]]
        first.append(selection(near[:, :, 0].transpose(3, 1, 0, 2), 256))
        second.append(selection(near[:, :, 1].transpose(3, 0, 2, 1), 256))
    return np.stack(first), np.stack(second)


def final_picks():
    at = np.arange(256).reshape(4, 8, 2, 2, 2)
    return np.stack(
        [
            selection(at[[yz ^ own for yz in range(4)]].transpose(4, 1, 2, 0, 3), 256)
            for own in range(4)
        ]
    )


FIRST, SECOND = phase_picks()
FINAL = final_picks()


def dot(a, b):
    return jnp.dot(a, b, preferred_element_type=F32)


def in_hbm(value):
    return pltpu.with_memory_space_constraint(value, pltpu.HBM)


def params(mebibytes):
    return pltpu.CompilerParams(vmem_limit_bytes=mebibytes * 1024 * 1024)


def rotate_kernel(place, w_hbm, a_hbm, mix_hbm, order_hbm, send0, send1, keep0, keep1, phases,
                  w_ref, a_ref, mix_ref, order_ref, waves, mixed, far, w_sems, sems):
    blocks = []
    for z, y, high in ((0, 0, 0), (1, 0, 0), (0, 0, 1), (0, 1, 1), (0, 1, 0), (1, 1, 0), (1, 0, 1), (1, 1, 1)):
        blocks.append(((place[0] ^ (1 - y)) * 2 + (place[1] ^ (1 - z)), high))
    small = [pltpu.make_async_copy(a_hbm.at[0], a_ref.at[0], sems.at[0])]
    small.append(pltpu.make_async_copy(mix_hbm, mix_ref, sems.at[1]))
    small.append(pltpu.make_async_copy(a_hbm.at[1:3], a_ref.at[1:3], sems.at[2]))
    small.append(pltpu.make_async_copy(order_hbm, order_ref, sems.at[3]))
    large = [
        pltpu.make_async_copy(w_hbm.at[:, at, 128 * high : 128 * high + 128], w_ref.at[j], w_sems.at[j])
        for j, (at, high) in enumerate(blocks)
    ]
    small[0].start()
    large[0].start()
    small[1].start()
    for copy in large[1:]:
        copy.start()
    small[2].start()
    small[3].start()
    small[0].wait()
    small[2].wait()
    small[3].wait()
    for j, (at, high) in enumerate(blocks):
        for x2 in range(2):
            for y in range(2):
                waves[j, x2, 0, 4 * y : 4 * y + 4, :] = a_ref[0, x2, at, 2 * high + y]
            sine, cosine = sin_cos(waves[j, x2, 0])
            waves[j, x2, 0] = sine
            waves[j, x2, 1] = cosine
    for j, (at, high) in enumerate(blocks):
        if j == 0:
            for copy in large:
                copy.wait()
            small[1].wait()
        for x2 in range(2):
            sine, cosine = waves[j, x2, 0], waves[j, x2, 1]
            for low in range(8):
                block = w_ref[j, x2, 16 * low : 16 * low + 16, :].astype(F32)
                re, im = block[:8], block[8:]
                s = sine[low : low + 1]
                c = cosine[low : low + 1]
                turned = jnp.concatenate([re * c - im * s, re * s + im * c], axis=0)
                row = 128 * x2 + 16 * low
                mixed[j, row : row + 16, :] = turned.astype(BF)
        (send0, send1, keep0, keep1)[j // 2][j % 2] = dot(mix_ref[...], mixed[j]).astype(BF)
    for block in range(4):
        for level in range(2):
            for x2 in range(2):
                for y in range(4):
                    row = 32 * level + 16 * x2 + 4 * y
                    far[block, row : row + 4, :] = a_ref[1 + level, x2, block, y]
        value = far[block].astype(BF)
        value = jnp.concatenate([value[:, :HALF], value[:, HALF:]], axis=0)
        value = dot(order_ref[...], value).astype(BF)
        for high in range(2):
            phases[high, block] = value[64 * high : 64 * high + 64]


def rotate(place, weights, angles):
    piece = jax.ShapeDtypeStruct((2, 256, CHEB), BF)
    return pl.pallas_call(
        rotate_kernel,
        out_shape=[piece] * 4 + [jax.ShapeDtypeStruct((2, 4, 64, HALF), BF)],
        in_specs=[pl.BlockSpec(memory_space=pltpu.SMEM)] + [pl.BlockSpec(memory_space=pl.ANY)] * 4,
        out_specs=[pl.BlockSpec(memory_space=pltpu.VMEM)] * 5,
        scratch_shapes=[
            pltpu.VMEM((8, 2, 128, CHEB), BF),
            pltpu.VMEM((3, 2, 4, 4, 4, CHEB), F32),
            pltpu.VMEM((256, 256), BF),
            pltpu.VMEM((128, 128), BF),
            pltpu.VMEM((8, 2, 2, 8, CHEB), F32),
            pltpu.VMEM((8, 256, CHEB), BF),
            pltpu.VMEM((4, 64, CHEB), F32),
            pltpu.SemaphoreType.DMA((8,)),
            pltpu.SemaphoreType.DMA((4,)),
        ],
        compiler_params=params(16),
        name="rotate",
    )(place, weights, angles, in_hbm(jnp.asarray(MIX, BF)), in_hbm(jnp.asarray(SEND_PHASE, BF)))


def add(a, b):
    return (a.astype(F32) + b.astype(F32)).astype(BF)


def sum_kernel(keep0, come0, again0, keep1, come1, again1, out_ref):
    for half, (kept, come, again) in enumerate(((keep0, come0, again0), (keep1, come1, again1))):
        out_ref[half] = add(add(kept[1], come[1]), again[...])


def sums(*args):
    return pl.pallas_call(
        sum_kernel,
        out_shape=jax.ShapeDtypeStruct((2, 256, CHEB), BF),
        in_specs=[pl.BlockSpec(memory_space=pltpu.VMEM)] * 6,
        out_specs=pl.BlockSpec(memory_space=pltpu.VMEM),
        compiler_params=params(8),
        name="sums",
    )(*args)


def trig_kernel(place, *refs):
    near1, near2 = refs[0:4], refs[4:8]
    first_ref, second_ref, out_ref = refs[8:]
    step = pl.program_id(0)

    def write(t, angle):
        for half in range(2):
            for at in range(0, 64, 8):
                sine, cosine = sin_cos(angle[64 * half + at : 64 * half + at + 8])
                out_ref[t, 0, at : at + 8, HALF * half : HALF * half + HALF] = sine
                out_ref[t, 1, at : at + 8, HALF * half : HALF * half + HALF] = cosine

    @pl.when(step < 2)
    def _():
        for t in range(4):
            held = jnp.concatenate([r[t] for r in near1], axis=0)
            write(t, dot(first_ref[0], held))

    @pl.when(step >= 2)
    def _():
        for t in range(4):
            held = [r[:, 8 * t : 8 * t + 8, :].astype(F32).reshape(64, HALF) for r in near2]
            write(t, dot(second_ref[0], jnp.concatenate(held, axis=0).astype(BF)))


def trig(place, near):
    def own(*shape):
        return pl.BlockSpec((1, *shape), lambda i, p: (p[2],) + (0,) * len(shape))

    spec = pltpu.PrefetchScalarGridSpec(
        num_scalar_prefetch=1,
        grid=(4,),
        in_specs=[pl.BlockSpec((4, 64, HALF), lambda i, p: (jnp.minimum(i, 1), 0, 0))] * 4
        + [pl.BlockSpec((8, 32, HALF), lambda i, p: (0, jnp.maximum(i - 2, 0), 0))] * 4
        + [own(128, 256), own(128, 256)],
        out_specs=pl.BlockSpec((4, 2, 64, CHEB), lambda i, p: (i, 0, 0, 0)),
    )
    return pl.pallas_call(
        trig_kernel,
        grid_spec=spec,
        out_shape=pltpu.HBM((16, 2, 64, CHEB), F32),
        compiler_params=params(12),
        cost_estimate=pl.CostEstimate(flops=7 * 10**9, bytes_accessed=10**6, transcendentals=0),
        name="trig",
    )(place, *near, *near, in_hbm(jnp.asarray(FIRST, BF)), in_hbm(jnp.asarray(SECOND, BF)))


def levels_kernel(x_ref, t_ref, trig_ref, enter_ref, turn_ref, leave_ref, out_ref, left, middle, even, odd):
    step = pl.program_id(0)

    @pl.when(step == 0)
    def _():
        total = (x_ref[0].astype(F32) + x_ref[1].astype(F32)).astype(BF)
        left[...] = dot(enter_ref[...], total).astype(BF)

    @pl.when(step == 2)
    def _():
        left[...] = dot(turn_ref[...], middle[...]).astype(BF)

    def turn_and_sum(product, at):
        total = [jnp.zeros((8, CHEB), F32)] * 4
        for outer in range(8):
            sine = trig_ref[at, 0, 8 * outer : 8 * outer + 8, :]
            cosine = trig_ref[at, 1, 8 * outer : 8 * outer + 8, :]
            for r in range(2):
                row = 32 * outer + 8 * r
                re = product[row : row + 8, :]
                im = product[row + 16 : row + 24, :]
                total[r] = total[r] + (re * cosine - im * sine)
                total[2 + r] = total[2 + r] + (re * sine + im * cosine)
        return jnp.concatenate(total, axis=0).astype(BF)

    def four_orientations(put):
        even[...] = dot(left[...], t_ref[0])
        for t in range(4):
            if t < 3:
                (odd, even)[t % 2][...] = dot(left[...], t_ref[t + 1])
            put(t, turn_and_sum((even, odd)[t % 2], t))

    @pl.when(step < 2)
    def _():
        def put(t, value):
            row = pl.multiple_of(128 * step + 32 * t, 32)
            middle[pl.ds(row, 32), :] = value

        four_orientations(put)

    @pl.when(step >= 2)
    def _():
        def put(t, value):
            value = jnp.concatenate([value[:, :HALF], value[:, HALF:]], axis=0)
            value = dot(leave_ref[...], value)
            for t4 in range(8):
                out_ref[t4, t] = value[8 * t4 : 8 * t4 + 8].astype(BF)

        four_orientations(put)


def levels(share, translation, waves):
    def const(*shape):
        return pl.BlockSpec(shape, lambda i: (0,) * len(shape))

    return pl.pallas_call(
        levels_kernel,
        grid=(4,),
        out_shape=jax.ShapeDtypeStruct((8, 8, 8, HALF), BF),
        in_specs=[
            const(2, 256, CHEB),
            pl.BlockSpec((4, CHEB, CHEB), lambda i: (i % 2, 0, 0)),
            pl.BlockSpec((4, 2, 64, CHEB), lambda i: (i, 0, 0, 0)),
            const(256, 256),
            const(256, 256),
            const(64, 64),
        ],
        out_specs=pl.BlockSpec((8, 4, 8, HALF), lambda i: (0, jnp.maximum(i - 2, 0), 0, 0)),
        scratch_shapes=[
            pltpu.VMEM((256, CHEB), BF),
            pltpu.VMEM((256, CHEB), BF),
            pltpu.VMEM((256, CHEB), F32),
            pltpu.VMEM((256, CHEB), F32),
        ],
        compiler_params=params(20),
        name="levels",
    )(share, in_hbm(translation), in_hbm(waves), jnp.asarray(ENTER, BF), jnp.asarray(TURN, BF), jnp.asarray(LEAVE, BF))


def final_kernel(place, n0, n1, n2, n3, pick_ref, t_ref, out_ref, left, made, sems):
    own = place[2]
    copies = []
    for block in range(4):
        for high in range(2):
            at = 128 * block + 64 * high
            held = jnp.concatenate([r[at : at + 64] for r in (n0, n1, n2, n3)], axis=0)
            value = dot(pick_ref[own], held)
            value = jnp.concatenate([value[:128], value[128:]], axis=1)
            left[block, 128 * high : 128 * high + 128, :] = value.astype(BF)
        for x2 in range(2):
            made[x2, block] = dot(left[block], t_ref[4 * x2 + own]).astype(BF)
            copies.append(
                pltpu.make_async_copy(made.at[x2, block], out_ref.at[x2, block], sems.at[x2, block])
            )
            copies[-1].start()
    for copy in copies:
        copy.wait()


def final(place, near, translation):
    vmem = pl.BlockSpec(memory_space=pltpu.VMEM)
    return pl.pallas_call(
        final_kernel,
        out_shape=jax.ShapeDtypeStruct((2, 4, 256, CHEB), BF),
        in_specs=[pl.BlockSpec(memory_space=pltpu.SMEM)] + [vmem] * 6,
        out_specs=pl.BlockSpec(memory_space=pl.ANY),
        scratch_shapes=[
            pltpu.VMEM((4, 256, CHEB), BF),
            pltpu.VMEM((2, 4, 256, CHEB), BF),
            pltpu.SemaphoreType.DMA((2, 4)),
        ],
        compiler_params=params(14),
        name="final",
    )(place, *near, jnp.asarray(FINAL, BF), translation)


def swap(value, axis):
    return lax.ppermute(value, axis, [(0, 1), (1, 0)])


def four(value):
    other = swap(value, "y2")
    return value, swap(value, "z2"), other, swap(other, "z2")


def exchange(value, axes):
    return lax.all_to_all(value, axes, split_axis=0, concat_axis=0, tiled=True)


def shards(weights, angles, translation):
    bit = lax.axis_index
    place = jnp.stack([bit("y4"), bit("z4"), 2 * bit("y2") + bit("z2")]).astype(jnp.int32)
    shape = weights.shape
    weights = in_hbm(weights.reshape(2, 4, 256, CHEB))
    angles = in_hbm(angles.reshape(3, 2, 4, 4, 4, CHEB))
    send0, send1, keep0, keep1, phases = rotate(place, weights, angles)
    come0, come1 = swap(send0, "y4"), swap(send1, "z4")
    phases = exchange(phases.reshape(64, 8, HALF), ("x4", "y4", "z4", "x3", "y3", "z3"))
    again0, again1 = add(keep0[0], come0[0]), add(keep1[0], come1[0])
    phases, _, _ = lax.optimization_barrier((phases, again0, again1))
    near = four(phases.reshape(8, 64, HALF))
    again0, again1 = swap(again0, "z4"), swap(again1, "y4")
    share = sums(keep0, come0, again0, keep1, come1, again1)
    share = exchange(share.reshape(64, 8, CHEB), ("x4", "x3", "y3", "z3", "y2", "z2"))
    waves = trig(place, near)
    done = levels(share.reshape(2, 256, CHEB), translation, waves)
    done = exchange(done.reshape(64, 8, HALF), ("y4", "z4", "x4", "x3", "y3", "z3"))
    near = four(done.reshape(512, HALF))
    return final(place, near, translation).reshape(shape)


def solution(mesh):
    fine = Mesh(mesh.devices.reshape((2,) * len(BITS)), BITS)
    x, y, z = BITS[:2], BITS[2:5], BITS[5:]
    return jax.shard_map(
        shards,
        mesh=fine,
        in_specs=(P(x, y, z, None, None, None), P(None, x, y, z, None), P()),
        out_specs=P(x, y, z, None, None, None),
        check_vma=False,
    )
```

```python
import jax
import jax.numpy as jnp
import numpy as np
from jax import lax
from jax.experimental import pallas as pl
from jax.experimental.pallas import tpu as pltpu
from jax.sharding import Mesh
from jax.sharding import PartitionSpec as P

BITS = ("x4", "x3", "y4", "y3", "y2", "z4", "z3", "z2")
CHEB = 512
HALF = 256
BF = jnp.bfloat16
F32 = jnp.float32

SIN = (1.0, -0.1666666567325592, 0.00833332072943449, -0.00019840527966152877, 2.753572516667191e-06,
       -2.472758353633253e-08, 1.3608578153245787e-10)
COS = (1.0, -0.49999988079071045, 0.04166648909449577, -0.0013887794921174645, 2.4769700758042745e-05,
       -2.707722615014063e-07, 1.7238451777146224e-09)


def sin_cos(angle):
    square = angle * angle
    sine, cosine = jnp.full_like(square, SIN[-1]), jnp.full_like(square, COS[-1])
    for s, c in zip(SIN[-2::-1], COS[-2::-1]):
        sine, cosine = sine * square + s, cosine * square + c
    return sine * angle, cosine


def selection(source, count):
    source = np.asarray(source).reshape(-1)
    matrix = np.zeros((source.size, count), np.float32)
    matrix[np.arange(source.size), source] = 1
    return matrix


def rows(dims, order):
    return np.arange(int(np.prod(dims))).reshape(dims).transpose(order)


MIX = selection(rows((2, 8, 2, 4, 2), (1, 3, 0, 2, 4)), 256)
SEND_PHASE = selection(rows((2, 2, 2, 16), (3, 1, 2, 0)), 128)
ENTER = selection(rows((8, 4, 2, 2, 2), (0, 3, 4, 1, 2)), 256)
TURN = selection(rows((8, 2, 2, 8), (3, 1, 2, 0)), 256)
LEAVE = selection(rows((2, 2, 2, 2, 2, 2), (4, 5, 3, 1, 2, 0)), 64)


def phase_picks():
    first, second = [], []
    at = np.arange(256).reshape(4, 8, 2, 2, 2)
    for own in range(4):
        near = at[[yz ^ own for yz in range(4)]]
        first.append(selection(near[:, :, 0].transpose(3, 1, 0, 2), 256))
        second.append(selection(near[:, :, 1].transpose(3, 0, 2, 1), 256))
    return np.stack(first), np.stack(second)


def final_picks():
    at = np.arange(256).reshape(4, 8, 2, 2, 2)
    return np.stack(
        [
            selection(at[[yz ^ own for yz in range(4)]].transpose(4, 1, 2, 0, 3), 256)
            for own in range(4)
        ]
    )


FIRST, SECOND = phase_picks()
FINAL = final_picks()


def dot(a, b):
    return jnp.dot(a, b, preferred_element_type=F32)


def in_hbm(value):
    return pltpu.with_memory_space_constraint(value, pltpu.HBM)


def params(mebibytes):
    return pltpu.CompilerParams(vmem_limit_bytes=mebibytes * 1024 * 1024)


def rotate_kernel(place, w_hbm, a_hbm, mix_hbm, order_hbm, send0, send1, keep0, keep1, phases,
                  w_ref, a_ref, mix_ref, order_ref, waves, mixed, far, w_sems, sems):
    blocks = []
    for z, y, high in ((0, 0, 0), (1, 0, 0), (0, 0, 1), (0, 1, 1), (0, 1, 0), (1, 1, 0), (1, 0, 1), (1, 1, 1)):
        blocks.append(((place[0] ^ (1 - y)) * 2 + (place[1] ^ (1 - z)), high))
    small = [pltpu.make_async_copy(a_hbm.at[0], a_ref.at[0], sems.at[0])]
    small.append(pltpu.make_async_copy(mix_hbm, mix_ref, sems.at[1]))
    small.append(pltpu.make_async_copy(a_hbm.at[1:3], a_ref.at[1:3], sems.at[2]))
    small.append(pltpu.make_async_copy(order_hbm, order_ref, sems.at[3]))
    large = [
        pltpu.make_async_copy(w_hbm.at[:, at, 128 * high : 128 * high + 128], w_ref.at[j], w_sems.at[j])
        for j, (at, high) in enumerate(blocks)
    ]
    small[0].start()
    large[0].start()
    small[1].start()
    for copy in large[1:]:
        copy.start()
    small[2].start()
    small[3].start()
    small[0].wait()
    small[2].wait()
    small[3].wait()
    for j, (at, high) in enumerate(blocks):
        for x2 in range(2):
            for y in range(2):
                waves[j, x2, 0, 4 * y : 4 * y + 4, :] = a_ref[0, x2, at, 2 * high + y]
            sine, cosine = sin_cos(waves[j, x2, 0])
            waves[j, x2, 0] = sine
            waves[j, x2, 1] = cosine
    for j, (at, high) in enumerate(blocks):
        if j == 0:
            for copy in large:
                copy.wait()
            small[1].wait()
        for x2 in range(2):
            sine, cosine = waves[j, x2, 0], waves[j, x2, 1]
            for low in range(8):
                block = w_ref[j, x2, 16 * low : 16 * low + 16, :].astype(F32)
                re, im = block[:8], block[8:]
                s = sine[low : low + 1]
                c = cosine[low : low + 1]
                turned = jnp.concatenate([re * c - im * s, re * s + im * c], axis=0)
                row = 128 * x2 + 16 * low
                mixed[j, row : row + 16, :] = turned.astype(BF)
        (send0, send1, keep0, keep1)[j // 2][j % 2] = dot(mix_ref[...], mixed[j]).astype(BF)
    for block in range(4):
        for level in range(2):
            for x2 in range(2):
                for y in range(4):
                    row = 32 * level + 16 * x2 + 4 * y
                    far[block, row : row + 4, :] = a_ref[1 + level, x2, block, y]
        value = far[block].astype(BF)
        value = jnp.concatenate([value[:, :HALF], value[:, HALF:]], axis=0)
        value = dot(order_ref[...], value).astype(BF)
        for high in range(2):
            phases[high, block] = value[64 * high : 64 * high + 64]


def rotate(place, weights, angles):
    piece = jax.ShapeDtypeStruct((2, 256, CHEB), BF)
    return pl.pallas_call(
        rotate_kernel,
        out_shape=[piece] * 4 + [jax.ShapeDtypeStruct((2, 4, 64, HALF), BF)],
        in_specs=[pl.BlockSpec(memory_space=pltpu.SMEM)] + [pl.BlockSpec(memory_space=pl.ANY)] * 4,
        out_specs=[pl.BlockSpec(memory_space=pltpu.VMEM)] * 5,
        scratch_shapes=[
            pltpu.VMEM((8, 2, 128, CHEB), BF),
            pltpu.VMEM((3, 2, 4, 4, 4, CHEB), F32),
            pltpu.VMEM((256, 256), BF),
            pltpu.VMEM((128, 128), BF),
            pltpu.VMEM((8, 2, 2, 8, CHEB), F32),
            pltpu.VMEM((8, 256, CHEB), BF),
            pltpu.VMEM((4, 64, CHEB), F32),
            pltpu.SemaphoreType.DMA((8,)),
            pltpu.SemaphoreType.DMA((4,)),
        ],
        compiler_params=params(16),
        name="rotate",
    )(place, weights, angles, in_hbm(jnp.asarray(MIX, BF)), in_hbm(jnp.asarray(SEND_PHASE, BF)))


def add(a, b):
    return (a.astype(F32) + b.astype(F32)).astype(BF)


def sum_kernel(keep0, come0, again0, keep1, come1, again1, out_ref):
    for half, (kept, come, again) in enumerate(((keep0, come0, again0), (keep1, come1, again1))):
        out_ref[half] = add(add(kept[1], come[1]), again[...])


def sums(*args):
    return pl.pallas_call(
        sum_kernel,
        out_shape=jax.ShapeDtypeStruct((2, 256, CHEB), BF),
        in_specs=[pl.BlockSpec(memory_space=pltpu.VMEM)] * 6,
        out_specs=pl.BlockSpec(memory_space=pltpu.VMEM),
        compiler_params=params(8),
        name="sums",
    )(*args)


def trig_kernel(place, *refs):
    near1, near2 = refs[0:4], refs[4:8]
    first_ref, second_ref, out1_ref, out2_ref = refs[8:]
    step = pl.program_id(0)

    def write(out_ref, t, angle):
        for half in range(2):
            for at in range(0, 64, 8):
                sine, cosine = sin_cos(angle[64 * half + at : 64 * half + at + 8])
                out_ref[t, 0, at : at + 8, HALF * half : HALF * half + HALF] = sine
                out_ref[t, 1, at : at + 8, HALF * half : HALF * half + HALF] = cosine

    @pl.when(step < 2)
    def _():
        for t in range(4):
            held = jnp.concatenate([r[t] for r in near1], axis=0)
            write(out1_ref, t, dot(first_ref[0], held))

    @pl.when(step >= 2)
    def _():
        for t in range(4):
            held = [r[:, 8 * t : 8 * t + 8, :].astype(F32).reshape(64, HALF) for r in near2]
            write(out2_ref, t, dot(second_ref[0], jnp.concatenate(held, axis=0).astype(BF)))


def trig(place, near):
    def own(*shape):
        return pl.BlockSpec((1, *shape), lambda i, p: (p[2],) + (0,) * len(shape))

    spec = pltpu.PrefetchScalarGridSpec(
        num_scalar_prefetch=1,
        grid=(4,),
        in_specs=[pl.BlockSpec((4, 64, HALF), lambda i, p: (jnp.minimum(i, 1), 0, 0))] * 4
        + [pl.BlockSpec((8, 32, HALF), lambda i, p: (0, jnp.maximum(i - 2, 0), 0))] * 4
        + [own(128, 256), own(128, 256)],
        out_specs=[
            pl.BlockSpec((4, 2, 64, CHEB), lambda i, p: (jnp.minimum(i, 1), 0, 0, 0)),
            pl.BlockSpec((4, 2, 64, CHEB), lambda i, p: (jnp.maximum(i - 2, 0), 0, 0, 0)),
        ],
    )
    return pl.pallas_call(
        trig_kernel,
        grid_spec=spec,
        out_shape=[jax.ShapeDtypeStruct((8, 2, 64, CHEB), F32), pltpu.HBM((8, 2, 64, CHEB), F32)],
        compiler_params=params(14),
        cost_estimate=pl.CostEstimate(flops=7 * 10**9, bytes_accessed=10**6, transcendentals=0),
        name="trig",
    )(place, *near, *near, in_hbm(jnp.asarray(FIRST, BF)), in_hbm(jnp.asarray(SECOND, BF)))


def levels_kernel(place, x_ref, t_hbm, wave1_ref, wave2_hbm, enter_ref, turn_ref, leave_ref, out_ref, last_ref,
                  t_ref, wave2_ref, left, middle, even, odd, sems):
    matrices = [pltpu.make_async_copy(t_hbm.at[t], t_ref.at[t], sems.at[t]) for t in range(8)]
    waves = pltpu.make_async_copy(wave2_hbm, wave2_ref, sems.at[8])
    for copy in matrices:
        copy.start()
    waves.start()
    total = (x_ref[0].astype(F32) + x_ref[1].astype(F32)).astype(BF)
    left[...] = dot(enter_ref[...], total).astype(BF)

    def turn_and_sum(product, wave_ref, at):
        total = [jnp.zeros((8, CHEB), F32)] * 4
        for outer in range(8):
            sine = wave_ref[at, 0, 8 * outer : 8 * outer + 8, :]
            cosine = wave_ref[at, 1, 8 * outer : 8 * outer + 8, :]
            for r in range(2):
                row = 32 * outer + 8 * r
                re = product[row : row + 8, :]
                im = product[row + 16 : row + 24, :]
                total[r] = total[r] + (re * cosine - im * sine)
                total[2 + r] = total[2 + r] + (re * sine + im * cosine)
        return jnp.concatenate(total, axis=0).astype(BF)

    slots = (even, odd)
    for copy in matrices[:2]:
        copy.wait()
    even[...] = dot(left[...], t_ref[0])
    for t in range(8):
        if t % 2 == 1:
            for copy in matrices[t + 1 : t + 3]:
                copy.wait()
        if t < 7:
            slots[(t + 1) % 2][...] = dot(left[...], t_ref[t + 1])
        middle[32 * t : 32 * t + 32, :] = turn_and_sum(slots[t % 2], wave1_ref, t)
    waves.wait()
    kept = [
        pltpu.make_async_copy(t_ref.at[4 * x2 + place[2]], last_ref.at[x2], sems.at[9 + x2]) for x2 in range(2)
    ]
    for copy in kept:
        copy.start()
    left[...] = dot(turn_ref[...], middle[...]).astype(BF)

    def four_orientations(group, carry):
        even[...] = dot(left[...], t_ref[4 * group])
        for i in range(4):
            if i < 3:
                slots[(i + 1) % 2][...] = dot(left[...], t_ref[4 * group + i + 1])
            value = turn_and_sum(slots[i % 2], wave2_ref, 4 * group + i)
            value = jnp.concatenate([value[:, :HALF], value[:, HALF:]], axis=0)
            value = dot(leave_ref[...], value)
            for t4 in range(8):
                out_ref[t4, 4 * group + i] = value[8 * t4 : 8 * t4 + 8].astype(BF)
        return carry

    lax.fori_loop(0, 2, four_orientations, 0)
    for copy in kept:
        copy.wait()


def levels(place, share, translation, wave1, wave2):
    vmem, hbm = pl.BlockSpec(memory_space=pltpu.VMEM), pl.BlockSpec(memory_space=pl.ANY)
    return pl.pallas_call(
        levels_kernel,
        out_shape=[
            jax.ShapeDtypeStruct((8, 8, 8, HALF), BF),
            jax.ShapeDtypeStruct((2, CHEB, CHEB), BF),
        ],
        in_specs=[pl.BlockSpec(memory_space=pltpu.SMEM), vmem, hbm, vmem, hbm, vmem, vmem, vmem],
        out_specs=[vmem, vmem],
        scratch_shapes=[
            pltpu.VMEM((8, CHEB, CHEB), BF),
            pltpu.VMEM((8, 2, 64, CHEB), F32),
            pltpu.VMEM((256, CHEB), BF),
            pltpu.VMEM((256, CHEB), BF),
            pltpu.VMEM((256, CHEB), F32),
            pltpu.VMEM((256, CHEB), F32),
            pltpu.SemaphoreType.DMA((11,)),
        ],
        compiler_params=params(20),
        name="levels",
    )(
        place,
        share,
        in_hbm(translation),
        wave1,
        in_hbm(wave2),
        jnp.asarray(ENTER, BF),
        jnp.asarray(TURN, BF),
        jnp.asarray(LEAVE, BF),
    )


def final_kernel(place, n0, n1, n2, n3, pick_ref, t_ref, out_ref, left, made, sems):
    own = place[2]
    copies = []
    for block in range(4):
        for high in range(2):
            at = 128 * block + 64 * high
            held = jnp.concatenate([r[at : at + 64] for r in (n0, n1, n2, n3)], axis=0)
            value = dot(pick_ref[own], held)
            value = jnp.concatenate([value[:128], value[128:]], axis=1)
            left[block, 128 * high : 128 * high + 128, :] = value.astype(BF)
        for x2 in range(2):
            made[x2, block] = dot(left[block], t_ref[x2]).astype(BF)
            copies.append(
                pltpu.make_async_copy(made.at[x2, block], out_ref.at[x2, block], sems.at[x2, block])
            )
            copies[-1].start()
    for copy in copies:
        copy.wait()


def final(place, near, last):
    vmem = pl.BlockSpec(memory_space=pltpu.VMEM)
    return pl.pallas_call(
        final_kernel,
        out_shape=jax.ShapeDtypeStruct((2, 4, 256, CHEB), BF),
        in_specs=[pl.BlockSpec(memory_space=pltpu.SMEM)] + [vmem] * 6,
        out_specs=pl.BlockSpec(memory_space=pl.ANY),
        scratch_shapes=[
            pltpu.VMEM((4, 256, CHEB), BF),
            pltpu.VMEM((2, 4, 256, CHEB), BF),
            pltpu.SemaphoreType.DMA((2, 4)),
        ],
        compiler_params=params(14),
        name="final",
    )(place, *near, jnp.asarray(FINAL, BF), last)


def swap(value, axis):
    return lax.ppermute(value, axis, [(0, 1), (1, 0)])


def four(value):
    other = swap(value, "y2")
    return value, swap(value, "z2"), other, swap(other, "z2")


def exchange(value, axes):
    return lax.all_to_all(value, axes, split_axis=0, concat_axis=0, tiled=True)


def shards(weights, angles, translation):
    bit = lax.axis_index
    place = jnp.stack([bit("y4"), bit("z4"), 2 * bit("y2") + bit("z2")]).astype(jnp.int32)
    shape = weights.shape
    weights = in_hbm(weights.reshape(2, 4, 256, CHEB))
    angles = in_hbm(angles.reshape(3, 2, 4, 4, 4, CHEB))
    send0, send1, keep0, keep1, phases = rotate(place, weights, angles)
    come0, come1 = swap(send0, "y4"), swap(send1, "z4")
    phases = exchange(phases.reshape(64, 8, HALF), ("x4", "y4", "z4", "x3", "y3", "z3"))
    again0, again1 = add(keep0[0], come0[0]), add(keep1[0], come1[0])
    phases, _, _ = lax.optimization_barrier((phases, again0, again1))
    near = four(phases.reshape(8, 64, HALF))
    again0, again1 = swap(again0, "z4"), swap(again1, "y4")
    share = sums(keep0, come0, again0, keep1, come1, again1)
    share = exchange(share.reshape(64, 8, CHEB), ("x4", "x3", "y3", "z3", "y2", "z2"))
    wave1, wave2 = trig(place, near)
    done, last = levels(place, share.reshape(2, 256, CHEB), translation, wave1, wave2)
    done = exchange(done.reshape(64, 8, HALF), ("y4", "z4", "x4", "x3", "y3", "z3"))
    near = four(done.reshape(512, HALF))
    return final(place, near, last).reshape(shape)


def solution(mesh):
    fine = Mesh(mesh.devices.reshape((2,) * len(BITS)), BITS)
    x, y, z = BITS[:2], BITS[2:5], BITS[5:]
    return jax.shard_map(
        shards,
        mesh=fine,
        in_specs=(P(x, y, z, None, None, None), P(None, x, y, z, None), P()),
        out_specs=P(x, y, z, None, None, None),
        check_vma=False,
    )
```

```python
import jax
import jax.numpy as jnp
import numpy as np
from jax import lax
from jax.experimental import pallas as pl
from jax.experimental.pallas import tpu as pltpu
from jax.sharding import Mesh
from jax.sharding import PartitionSpec as P

BITS = ("x4", "x3", "y4", "y3", "y2", "z4", "z3", "z2")
CHEB = 512
HALF = 256
BF = jnp.bfloat16
F32 = jnp.float32

SIN = (1.0, -0.1666666567325592, 0.00833332072943449, -0.00019840527966152877, 2.753572516667191e-06,
       -2.472758353633253e-08, 1.3608578153245787e-10)
COS = (1.0, -0.49999988079071045, 0.04166648909449577, -0.0013887794921174645, 2.4769700758042745e-05,
       -2.707722615014063e-07, 1.7238451777146224e-09)


def sin_cos(angle):
    square = angle * angle
    sine, cosine = jnp.full_like(square, SIN[-1]), jnp.full_like(square, COS[-1])
    for s, c in zip(SIN[-2::-1], COS[-2::-1]):
        sine, cosine = sine * square + s, cosine * square + c
    return sine * angle, cosine


def selection(source, count):
    source = np.asarray(source).reshape(-1)
    matrix = np.zeros((source.size, count), np.float32)
    matrix[np.arange(source.size), source] = 1
    return matrix


def rows(dims, order):
    return np.arange(int(np.prod(dims))).reshape(dims).transpose(order)


MIX = selection(rows((2, 8, 2, 4, 2), (1, 3, 0, 2, 4)), 256)
SEND_PHASE = selection(rows((2, 2, 2, 16), (3, 1, 2, 0)), 128)
ENTER = selection(rows((8, 4, 2, 2, 2), (0, 3, 4, 1, 2)), 256)
TURN = selection(rows((8, 2, 2, 8), (3, 1, 2, 0)), 256)
LEAVE = selection(rows((2, 2, 2, 2, 2, 2), (4, 5, 3, 1, 2, 0)), 64)


def phase_picks():
    first, second = [], []
    at = np.arange(256).reshape(4, 8, 2, 2, 2)
    for own in range(4):
        near = at[[yz ^ own for yz in range(4)]]
        first.append(selection(near[:, :, 0].transpose(3, 1, 0, 2), 256))
        second.append(selection(near[:, :, 1].transpose(3, 0, 2, 1), 256))
    return np.stack(first), np.stack(second)


def final_picks():
    at = np.arange(256).reshape(4, 8, 2, 2, 2)
    return np.stack(
        [
            selection(at[[yz ^ own for yz in range(4)]].transpose(4, 1, 2, 0, 3), 256)
            for own in range(4)
        ]
    )


FIRST, SECOND = phase_picks()
FINAL = final_picks()


def dot(a, b):
    return jnp.dot(a, b, preferred_element_type=F32)


def in_hbm(value):
    return pltpu.with_memory_space_constraint(value, pltpu.HBM)


def params(mebibytes):
    return pltpu.CompilerParams(vmem_limit_bytes=mebibytes * 1024 * 1024)


def rotate_kernel(place, w_hbm, a_hbm, mix_hbm, order_hbm, send0, send1, keep0, keep1, phases,
                  w_ref, a_ref, mix_ref, order_ref, waves, mixed, far, w_sems, sems):
    blocks = []
    for z, y, high in ((0, 0, 0), (1, 0, 0), (0, 0, 1), (0, 1, 1), (0, 1, 0), (1, 1, 0), (1, 0, 1), (1, 1, 1)):
        blocks.append(((place[0] ^ (1 - y)) * 2 + (place[1] ^ (1 - z)), high))
    small = [pltpu.make_async_copy(a_hbm.at[0], a_ref.at[0], sems.at[0])]
    small.append(pltpu.make_async_copy(mix_hbm, mix_ref, sems.at[1]))
    small.append(pltpu.make_async_copy(a_hbm.at[1:3], a_ref.at[1:3], sems.at[2]))
    small.append(pltpu.make_async_copy(order_hbm, order_ref, sems.at[3]))
    large = [
        pltpu.make_async_copy(w_hbm.at[:, at, 128 * high : 128 * high + 128], w_ref.at[j], w_sems.at[j])
        for j, (at, high) in enumerate(blocks)
    ]
    small[0].start()
    large[0].start()
    small[1].start()
    for copy in large[1:]:
        copy.start()
    small[2].start()
    small[3].start()
    small[0].wait()
    small[2].wait()
    small[3].wait()
    for j, (at, high) in enumerate(blocks):
        for x2 in range(2):
            for y in range(2):
                waves[j, x2, 0, 4 * y : 4 * y + 4, :] = a_ref[0, x2, at, 2 * high + y]
            sine, cosine = sin_cos(waves[j, x2, 0])
            waves[j, x2, 0] = sine
            waves[j, x2, 1] = cosine
    for j, (at, high) in enumerate(blocks):
        if j == 0:
            for copy in large:
                copy.wait()
            small[1].wait()
        for x2 in range(2):
            sine, cosine = waves[j, x2, 0], waves[j, x2, 1]
            for low in range(8):
                block = w_ref[j, x2, 16 * low : 16 * low + 16, :].astype(F32)
                re, im = block[:8], block[8:]
                s = sine[low : low + 1]
                c = cosine[low : low + 1]
                turned = jnp.concatenate([re * c - im * s, re * s + im * c], axis=0)
                row = 128 * x2 + 16 * low
                mixed[j, row : row + 16, :] = turned.astype(BF)
        (send0, send1, keep0, keep1)[j // 2][j % 2] = dot(mix_ref[...], mixed[j]).astype(BF)
    for block in range(4):
        for level in range(2):
            for x2 in range(2):
                for y in range(4):
                    row = 32 * level + 16 * x2 + 4 * y
                    far[block, row : row + 4, :] = a_ref[1 + level, x2, block, y]
        value = far[block].astype(BF)
        value = jnp.concatenate([value[:, :HALF], value[:, HALF:]], axis=0)
        value = dot(order_ref[...], value).astype(BF)
        for high in range(2):
            phases[high, block] = value[64 * high : 64 * high + 64]


def rotate(place, weights, angles):
    piece = jax.ShapeDtypeStruct((2, 256, CHEB), BF)
    return pl.pallas_call(
        rotate_kernel,
        out_shape=[piece] * 4 + [jax.ShapeDtypeStruct((2, 4, 64, HALF), BF)],
        in_specs=[pl.BlockSpec(memory_space=pltpu.SMEM)] + [pl.BlockSpec(memory_space=pl.ANY)] * 4,
        out_specs=[pl.BlockSpec(memory_space=pltpu.VMEM)] * 5,
        scratch_shapes=[
            pltpu.VMEM((8, 2, 128, CHEB), BF),
            pltpu.VMEM((3, 2, 4, 4, 4, CHEB), F32),
            pltpu.VMEM((256, 256), BF),
            pltpu.VMEM((128, 128), BF),
            pltpu.VMEM((8, 2, 2, 8, CHEB), F32),
            pltpu.VMEM((8, 256, CHEB), BF),
            pltpu.VMEM((4, 64, CHEB), F32),
            pltpu.SemaphoreType.DMA((8,)),
            pltpu.SemaphoreType.DMA((4,)),
        ],
        compiler_params=params(16),
        name="rotate",
    )(place, weights, angles, in_hbm(jnp.asarray(MIX, BF)), in_hbm(jnp.asarray(SEND_PHASE, BF)))


def add(a, b):
    return (a.astype(F32) + b.astype(F32)).astype(BF)


def first_kernel(kept, come, out_ref):
    out_ref[...] = add(kept[0], come[0])


def first_sum(kept, come):
    return pl.pallas_call(
        first_kernel,
        out_shape=jax.ShapeDtypeStruct((256, CHEB), BF),
        in_specs=[pl.BlockSpec(memory_space=pltpu.VMEM)] * 2,
        out_specs=pl.BlockSpec(memory_space=pltpu.VMEM),
        compiler_params=params(8),
        name="first_sum",
    )(kept, come)


def sum_kernel(keep0, come0, again0, keep1, come1, again1, out_ref):
    for half, (kept, come, again) in enumerate(((keep0, come0, again0), (keep1, come1, again1))):
        out_ref[half] = add(add(kept[1], come[1]), again[...])


def sums(*args):
    return pl.pallas_call(
        sum_kernel,
        out_shape=jax.ShapeDtypeStruct((2, 256, CHEB), BF),
        in_specs=[pl.BlockSpec(memory_space=pltpu.VMEM)] * 6,
        out_specs=pl.BlockSpec(memory_space=pltpu.VMEM),
        compiler_params=params(8),
        name="sums",
    )(*args)


def trig_kernel(place, *refs):
    near1, near2 = refs[0:4], refs[4:8]
    first_ref, second_ref, out1_ref, out2_ref = refs[8:]
    step = pl.program_id(0)

    def write(out_ref, t, angle):
        for half in range(2):
            for at in range(0, 64, 8):
                sine, cosine = sin_cos(angle[64 * half + at : 64 * half + at + 8])
                out_ref[t, 0, at : at + 8, HALF * half : HALF * half + HALF] = sine
                out_ref[t, 1, at : at + 8, HALF * half : HALF * half + HALF] = cosine

    @pl.when(step < 2)
    def _():
        for t in range(4):
            held = jnp.concatenate([r[t] for r in near1], axis=0)
            write(out1_ref, t, dot(first_ref[0], held))

    @pl.when(step >= 2)
    def _():
        for t in range(4):
            held = [r[:, 8 * t : 8 * t + 8, :].astype(F32).reshape(64, HALF) for r in near2]
            write(out2_ref, t, dot(second_ref[0], jnp.concatenate(held, axis=0).astype(BF)))


def trig(place, near):
    def own(*shape):
        return pl.BlockSpec((1, *shape), lambda i, p: (p[2],) + (0,) * len(shape))

    spec = pltpu.PrefetchScalarGridSpec(
        num_scalar_prefetch=1,
        grid=(4,),
        in_specs=[pl.BlockSpec((4, 64, HALF), lambda i, p: (jnp.minimum(i, 1), 0, 0))] * 4
        + [pl.BlockSpec((8, 32, HALF), lambda i, p: (0, jnp.maximum(i - 2, 0), 0))] * 4
        + [own(128, 256), own(128, 256)],
        out_specs=[
            pl.BlockSpec((4, 2, 64, CHEB), lambda i, p: (jnp.minimum(i, 1), 0, 0, 0)),
            pl.BlockSpec((4, 2, 64, CHEB), lambda i, p: (jnp.maximum(i - 2, 0), 0, 0, 0)),
        ],
    )
    return pl.pallas_call(
        trig_kernel,
        grid_spec=spec,
        out_shape=[jax.ShapeDtypeStruct((8, 2, 64, CHEB), F32), pltpu.HBM((8, 2, 64, CHEB), F32)],
        compiler_params=params(14),
        cost_estimate=pl.CostEstimate(flops=7 * 10**9, bytes_accessed=10**6, transcendentals=0),
        name="trig",
    )(place, *near, *near, in_hbm(jnp.asarray(FIRST, BF)), in_hbm(jnp.asarray(SECOND, BF)))


def levels_kernel(place, x_ref, t_hbm, wave1_ref, wave2_hbm, enter_ref, turn_ref, leave_ref, out_ref, last_ref,
                  t_ref, wave2_ref, left, middle, even, odd, sems):
    matrices = [pltpu.make_async_copy(t_hbm.at[t], t_ref.at[t], sems.at[t]) for t in range(8)]
    waves = pltpu.make_async_copy(wave2_hbm, wave2_ref, sems.at[8])
    for copy in matrices:
        copy.start()
    waves.start()
    total = (x_ref[0].astype(F32) + x_ref[1].astype(F32)).astype(BF)
    left[...] = dot(enter_ref[...], total).astype(BF)

    def turn_and_sum(product, wave_ref, at):
        total = [jnp.zeros((8, CHEB), F32)] * 4
        for outer in range(8):
            sine = wave_ref[at, 0, 8 * outer : 8 * outer + 8, :]
            cosine = wave_ref[at, 1, 8 * outer : 8 * outer + 8, :]
            for r in range(2):
                row = 32 * outer + 8 * r
                re = product[row : row + 8, :]
                im = product[row + 16 : row + 24, :]
                total[r] = total[r] + (re * cosine - im * sine)
                total[2 + r] = total[2 + r] + (re * sine + im * cosine)
        return jnp.concatenate(total, axis=0).astype(BF)

    slots = (even, odd)
    for copy in matrices[:2]:
        copy.wait()
    even[...] = dot(left[...], t_ref[0])
    for t in range(8):
        if t % 2 == 1:
            for copy in matrices[t + 1 : t + 3]:
                copy.wait()
        if t < 7:
            slots[(t + 1) % 2][...] = dot(left[...], t_ref[t + 1])
        middle[32 * t : 32 * t + 32, :] = turn_and_sum(slots[t % 2], wave1_ref, t)
    waves.wait()
    kept = [
        pltpu.make_async_copy(t_ref.at[4 * x2 + place[2]], last_ref.at[x2], sems.at[9 + x2]) for x2 in range(2)
    ]
    for copy in kept:
        copy.start()
    left[...] = dot(turn_ref[...], middle[...]).astype(BF)

    def four_orientations(group, carry):
        even[...] = dot(left[...], t_ref[4 * group])
        for i in range(4):
            if i < 3:
                slots[(i + 1) % 2][...] = dot(left[...], t_ref[4 * group + i + 1])
            value = turn_and_sum(slots[i % 2], wave2_ref, 4 * group + i)
            value = jnp.concatenate([value[:, :HALF], value[:, HALF:]], axis=0)
            value = dot(leave_ref[...], value)
            for t4 in range(8):
                out_ref[t4, 4 * group + i] = value[8 * t4 : 8 * t4 + 8].astype(BF)
        return carry

    lax.fori_loop(0, 2, four_orientations, 0)
    for copy in kept:
        copy.wait()


def levels(place, share, translation, wave1, wave2):
    vmem, hbm = pl.BlockSpec(memory_space=pltpu.VMEM), pl.BlockSpec(memory_space=pl.ANY)
    return pl.pallas_call(
        levels_kernel,
        out_shape=[
            jax.ShapeDtypeStruct((8, 8, 8, HALF), BF),
            jax.ShapeDtypeStruct((2, CHEB, CHEB), BF),
        ],
        in_specs=[pl.BlockSpec(memory_space=pltpu.SMEM), vmem, hbm, vmem, hbm, vmem, vmem, vmem],
        out_specs=[vmem, vmem],
        scratch_shapes=[
            pltpu.VMEM((8, CHEB, CHEB), BF),
            pltpu.VMEM((8, 2, 64, CHEB), F32),
            pltpu.VMEM((256, CHEB), BF),
            pltpu.VMEM((256, CHEB), BF),
            pltpu.VMEM((256, CHEB), F32),
            pltpu.VMEM((256, CHEB), F32),
            pltpu.SemaphoreType.DMA((11,)),
        ],
        compiler_params=params(20),
        name="levels",
    )(
        place,
        share,
        in_hbm(translation),
        wave1,
        in_hbm(wave2),
        jnp.asarray(ENTER, BF),
        jnp.asarray(TURN, BF),
        jnp.asarray(LEAVE, BF),
    )


def final_kernel(place, n0, n1, n2, n3, pick_ref, t_ref, out_ref, left, made, sems):
    own = place[2]
    copies = []
    for block in range(4):
        for high in range(2):
            at = 128 * block + 64 * high
            held = jnp.concatenate([r[at : at + 64] for r in (n0, n1, n2, n3)], axis=0)
            value = dot(pick_ref[own], held)
            value = jnp.concatenate([value[:128], value[128:]], axis=1)
            left[block, 128 * high : 128 * high + 128, :] = value.astype(BF)
        for x2 in range(2):
            made[x2, block] = dot(left[block], t_ref[x2]).astype(BF)
            copies.append(
                pltpu.make_async_copy(made.at[x2, block], out_ref.at[x2, block], sems.at[x2, block])
            )
            copies[-1].start()
    for copy in copies:
        copy.wait()


def final(place, near, last):
    vmem = pl.BlockSpec(memory_space=pltpu.VMEM)
    return pl.pallas_call(
        final_kernel,
        out_shape=jax.ShapeDtypeStruct((2, 4, 256, CHEB), BF),
        in_specs=[pl.BlockSpec(memory_space=pltpu.SMEM)] + [vmem] * 6,
        out_specs=pl.BlockSpec(memory_space=pl.ANY),
        scratch_shapes=[
            pltpu.VMEM((4, 256, CHEB), BF),
            pltpu.VMEM((2, 4, 256, CHEB), BF),
            pltpu.SemaphoreType.DMA((2, 4)),
        ],
        compiler_params=params(14),
        name="final",
    )(place, *near, jnp.asarray(FINAL, BF), last)


def swap(value, axis):
    return lax.ppermute(value, axis, [(0, 1), (1, 0)])


def four(value):
    other = swap(value, "y2")
    return value, swap(value, "z2"), other, swap(other, "z2")


def exchange(value, axes):
    return lax.all_to_all(value, axes, split_axis=0, concat_axis=0, tiled=True)


def shards(weights, angles, translation):
    bit = lax.axis_index
    place = jnp.stack([bit("y4"), bit("z4"), 2 * bit("y2") + bit("z2")]).astype(jnp.int32)
    shape = weights.shape
    weights = in_hbm(weights.reshape(2, 4, 256, CHEB))
    angles = in_hbm(angles.reshape(3, 2, 4, 4, 4, CHEB))
    send0, send1, keep0, keep1, phases = rotate(place, weights, angles)
    come0, come1 = swap(send0, "y4"), swap(send1, "z4")
    phases = exchange(phases.reshape(64, 8, HALF), ("x4", "y4", "z4", "x3", "y3", "z3"))
    again0, again1 = first_sum(keep0, come0), first_sum(keep1, come1)
    again0, again1 = swap(again0, "z4"), swap(again1, "y4")
    share = sums(keep0, come0, again0, keep1, come1, again1)
    phases, _ = lax.optimization_barrier((phases, share))
    near = four(phases.reshape(8, 64, HALF))
    share = exchange(share.reshape(64, 8, CHEB), ("x4", "x3", "y3", "z3", "y2", "z2"))
    wave1, wave2 = trig(place, near)
    done, last = levels(place, share.reshape(2, 256, CHEB), translation, wave1, wave2)
    done = exchange(done.reshape(64, 8, HALF), ("y4", "z4", "x4", "x3", "y3", "z3"))
    near = four(done.reshape(512, HALF))
    return final(place, near, last).reshape(shape)


def solution(mesh):
    fine = Mesh(mesh.devices.reshape((2,) * len(BITS)), BITS)
    x, y, z = BITS[:2], BITS[2:5], BITS[5:]
    return jax.shard_map(
        shards,
        mesh=fine,
        in_specs=(P(x, y, z, None, None, None), P(None, x, y, z, None), P()),
        out_specs=P(x, y, z, None, None, None),
        check_vma=False,
    )
```

```python
import jax
import jax.numpy as jnp
import numpy as np
from jax import lax
from jax.experimental import pallas as pl
from jax.experimental.pallas import tpu as pltpu
from jax.sharding import Mesh
from jax.sharding import PartitionSpec as P

BITS = ("x4", "x3", "y4", "y3", "y2", "z4", "z3", "z2")
CHEB = 512
HALF = 256
BF = jnp.bfloat16
F32 = jnp.float32

SIN = (1.0, -0.1666666567325592, 0.00833332072943449, -0.00019840527966152877, 2.753572516667191e-06,
       -2.472758353633253e-08, 1.3608578153245787e-10)
COS = (1.0, -0.49999988079071045, 0.04166648909449577, -0.0013887794921174645, 2.4769700758042745e-05,
       -2.707722615014063e-07, 1.7238451777146224e-09)


def sin_cos(angle):
    square = angle * angle
    sine, cosine = jnp.full_like(square, SIN[-1]), jnp.full_like(square, COS[-1])
    for s, c in zip(SIN[-2::-1], COS[-2::-1]):
        sine, cosine = sine * square + s, cosine * square + c
    return sine * angle, cosine


def selection(source, count):
    source = np.asarray(source).reshape(-1)
    matrix = np.zeros((source.size, count), np.float32)
    matrix[np.arange(source.size), source] = 1
    return matrix


def rows(dims, order):
    return np.arange(int(np.prod(dims))).reshape(dims).transpose(order)


MIX = selection(rows((2, 8, 2, 4, 2), (1, 3, 0, 2, 4)), 256)
SEND_PHASE = selection(rows((2, 2, 2, 16), (3, 1, 2, 0)), 128)
ENTER = selection(rows((8, 4, 2, 2, 2), (0, 3, 4, 1, 2)), 256)
TURN = selection(rows((8, 2, 2, 8), (3, 1, 2, 0)), 256)
LEAVE = selection(rows((2, 2, 2, 2, 2, 2), (4, 5, 3, 1, 2, 0)), 64)


def phase_picks():
    first, second = [], []
    at = np.arange(256).reshape(4, 8, 2, 2, 2)
    for own in range(4):
        near = at[[yz ^ own for yz in range(4)]]
        first.append(selection(near[:, :, 0].transpose(3, 1, 0, 2), 256))
        second.append(selection(near[:, :, 1].transpose(3, 0, 2, 1), 256))
    return np.stack(first), np.stack(second)


def final_picks():
    at = np.arange(256).reshape(4, 8, 2, 2, 2)
    return np.stack(
        [
            selection(at[[yz ^ own for yz in range(4)]].transpose(4, 1, 2, 0, 3), 256)
            for own in range(4)
        ]
    )


FIRST, SECOND = phase_picks()
FINAL = final_picks()


def dot(a, b):
    return jnp.dot(a, b, preferred_element_type=F32)


def in_hbm(value):
    return pltpu.with_memory_space_constraint(value, pltpu.HBM)


def params(mebibytes):
    return pltpu.CompilerParams(vmem_limit_bytes=mebibytes * 1024 * 1024)


def rotate_kernel(place, w_hbm, a_hbm, mix_hbm, order_hbm, send0, send1, keep0, keep1, phases,
                  w_ref, a_ref, mix_ref, order_ref, waves, mixed, far, w_sems, sems):
    blocks = []
    for z, y, high in ((0, 0, 0), (1, 0, 0), (0, 0, 1), (0, 1, 1), (0, 1, 0), (1, 1, 0), (1, 0, 1), (1, 1, 1)):
        blocks.append(((place[0] ^ (1 - y)) * 2 + (place[1] ^ (1 - z)), high))
    small = [pltpu.make_async_copy(a_hbm.at[0], a_ref.at[0], sems.at[0])]
    small.append(pltpu.make_async_copy(mix_hbm, mix_ref, sems.at[1]))
    small.append(pltpu.make_async_copy(a_hbm.at[1:3], a_ref.at[1:3], sems.at[2]))
    small.append(pltpu.make_async_copy(order_hbm, order_ref, sems.at[3]))
    large = [
        pltpu.make_async_copy(w_hbm.at[:, at, 128 * high : 128 * high + 128], w_ref.at[j], w_sems.at[j])
        for j, (at, high) in enumerate(blocks)
    ]
    small[0].start()
    large[0].start()
    small[1].start()
    for copy in large[1:]:
        copy.start()
    small[2].start()
    small[3].start()
    small[0].wait()
    small[2].wait()
    small[3].wait()
    for j, (at, high) in enumerate(blocks):
        for x2 in range(2):
            for y in range(2):
                waves[j, x2, 0, 4 * y : 4 * y + 4, :] = a_ref[0, x2, at, 2 * high + y]
            sine, cosine = sin_cos(waves[j, x2, 0])
            waves[j, x2, 0] = sine
            waves[j, x2, 1] = cosine
    for j, (at, high) in enumerate(blocks):
        if j == 0:
            for copy in large:
                copy.wait()
            small[1].wait()
        for x2 in range(2):
            sine, cosine = waves[j, x2, 0], waves[j, x2, 1]
            for low in range(8):
                block = w_ref[j, x2, 16 * low : 16 * low + 16, :].astype(F32)
                re, im = block[:8], block[8:]
                s = sine[low : low + 1]
                c = cosine[low : low + 1]
                turned = jnp.concatenate([re * c - im * s, re * s + im * c], axis=0)
                row = 128 * x2 + 16 * low
                mixed[j, row : row + 16, :] = turned.astype(BF)
        (send0, send1, keep0, keep1)[j // 2][j % 2] = dot(mix_ref[...], mixed[j]).astype(BF)
    for block in range(4):
        for level in range(2):
            for x2 in range(2):
                for y in range(4):
                    row = 32 * level + 16 * x2 + 4 * y
                    far[block, row : row + 4, :] = a_ref[1 + level, x2, block, y]
        value = far[block].astype(BF)
        value = jnp.concatenate([value[:, :HALF], value[:, HALF:]], axis=0)
        value = dot(order_ref[...], value).astype(BF)
        for high in range(2):
            phases[high, block] = value[64 * high : 64 * high + 64]


def rotate(place, weights, angles):
    piece = jax.ShapeDtypeStruct((2, 256, CHEB), BF)
    return pl.pallas_call(
        rotate_kernel,
        out_shape=[piece] * 4 + [jax.ShapeDtypeStruct((2, 4, 64, HALF), BF)],
        in_specs=[pl.BlockSpec(memory_space=pltpu.SMEM)] + [pl.BlockSpec(memory_space=pl.ANY)] * 4,
        out_specs=[pl.BlockSpec(memory_space=pltpu.VMEM)] * 5,
        scratch_shapes=[
            pltpu.VMEM((8, 2, 128, CHEB), BF),
            pltpu.VMEM((3, 2, 4, 4, 4, CHEB), F32),
            pltpu.VMEM((256, 256), BF),
            pltpu.VMEM((128, 128), BF),
            pltpu.VMEM((8, 2, 2, 8, CHEB), F32),
            pltpu.VMEM((8, 256, CHEB), BF),
            pltpu.VMEM((4, 64, CHEB), F32),
            pltpu.SemaphoreType.DMA((8,)),
            pltpu.SemaphoreType.DMA((4,)),
        ],
        compiler_params=params(16),
        name="rotate",
    )(place, weights, angles, in_hbm(jnp.asarray(MIX, BF)), in_hbm(jnp.asarray(SEND_PHASE, BF)))


def add(a, b):
    return (a.astype(F32) + b.astype(F32)).astype(BF)


def first_kernel(kept, come, out_ref):
    out_ref[...] = add(kept[0], come[0])


def first_sum(kept, come):
    return pl.pallas_call(
        first_kernel,
        out_shape=jax.ShapeDtypeStruct((256, CHEB), BF),
        in_specs=[pl.BlockSpec(memory_space=pltpu.VMEM)] * 2,
        out_specs=pl.BlockSpec(memory_space=pltpu.VMEM),
        compiler_params=params(8),
        name="first_sum",
    )(kept, come)


def sum_kernel(keep0, come0, again0, keep1, come1, again1, out_ref):
    for half, (kept, come, again) in enumerate(((keep0, come0, again0), (keep1, come1, again1))):
        out_ref[half] = add(add(kept[1], come[1]), again[...])


def sums(*args):
    return pl.pallas_call(
        sum_kernel,
        out_shape=jax.ShapeDtypeStruct((2, 256, CHEB), BF),
        in_specs=[pl.BlockSpec(memory_space=pltpu.VMEM)] * 6,
        out_specs=pl.BlockSpec(memory_space=pltpu.VMEM),
        compiler_params=params(8),
        name="sums",
    )(*args)


def trig_kernel(place, *refs):
    near1, near2 = refs[0:4], refs[4:8]
    first_ref, second_ref, out1_ref, out2_ref = refs[8:]
    step = pl.program_id(0)

    def write(out_ref, t, angle):
        for half in range(2):
            for at in range(0, 64, 8):
                sine, cosine = sin_cos(angle[64 * half + at : 64 * half + at + 8])
                out_ref[t, 0, at : at + 8, HALF * half : HALF * half + HALF] = sine
                out_ref[t, 1, at : at + 8, HALF * half : HALF * half + HALF] = cosine

    @pl.when(step < 2)
    def _():
        for t in range(4):
            held = jnp.concatenate([r[t] for r in near1], axis=0)
            write(out1_ref, t, dot(first_ref[0], held))

    @pl.when(step >= 2)
    def _():
        for t in range(4):
            held = [r[:, 8 * t : 8 * t + 8, :].astype(F32).reshape(64, HALF) for r in near2]
            write(out2_ref, t, dot(second_ref[0], jnp.concatenate(held, axis=0).astype(BF)))


def trig(place, near):
    def own(*shape):
        return pl.BlockSpec((1, *shape), lambda i, p: (p[2],) + (0,) * len(shape))

    spec = pltpu.PrefetchScalarGridSpec(
        num_scalar_prefetch=1,
        grid=(4,),
        in_specs=[pl.BlockSpec((4, 64, HALF), lambda i, p: (jnp.minimum(i, 1), 0, 0))] * 4
        + [pl.BlockSpec((8, 32, HALF), lambda i, p: (0, jnp.maximum(i - 2, 0), 0))] * 4
        + [own(128, 256), own(128, 256)],
        out_specs=[
            pl.BlockSpec((4, 2, 64, CHEB), lambda i, p: (jnp.minimum(i, 1), 0, 0, 0)),
            pl.BlockSpec((4, 2, 64, CHEB), lambda i, p: (jnp.maximum(i - 2, 0), 0, 0, 0)),
        ],
    )
    return pl.pallas_call(
        trig_kernel,
        grid_spec=spec,
        out_shape=[jax.ShapeDtypeStruct((8, 2, 64, CHEB), F32), pltpu.HBM((8, 2, 64, CHEB), F32)],
        compiler_params=params(14),
        cost_estimate=pl.CostEstimate(flops=7 * 10**9, bytes_accessed=10**6, transcendentals=0),
        name="trig",
    )(place, *near, *near, in_hbm(jnp.asarray(FIRST, BF)), in_hbm(jnp.asarray(SECOND, BF)))


def levels_kernel(place, x_ref, t_hbm, wave1_ref, wave2_hbm, enter_ref, turn_ref, leave_ref, out_ref, last_ref,
                  t_ref, wave2_ref, left, middle, even, odd, sems):
    matrices = [pltpu.make_async_copy(t_hbm.at[t], t_ref.at[t], sems.at[t]) for t in range(8)]
    waves = pltpu.make_async_copy(wave2_hbm, wave2_ref, sems.at[8])
    for copy in matrices:
        copy.start()
    waves.start()
    total = (x_ref[0].astype(F32) + x_ref[1].astype(F32)).astype(BF)
    left[...] = dot(enter_ref[...], total).astype(BF)

    def turn_and_sum(product, wave_ref, at):
        total = [jnp.zeros((8, CHEB), F32)] * 4
        for outer in range(8):
            sine = wave_ref[at, 0, 8 * outer : 8 * outer + 8, :]
            cosine = wave_ref[at, 1, 8 * outer : 8 * outer + 8, :]
            for r in range(2):
                row = 32 * outer + 8 * r
                re = product[row : row + 8, :]
                im = product[row + 16 : row + 24, :]
                total[r] = total[r] + (re * cosine - im * sine)
                total[2 + r] = total[2 + r] + (re * sine + im * cosine)
        return jnp.concatenate(total, axis=0).astype(BF)

    slots = (even, odd)
    for copy in matrices[:2]:
        copy.wait()
    even[...] = dot(left[...], t_ref[0])
    for t in range(8):
        if t % 2 == 1:
            for copy in matrices[t + 1 : t + 3]:
                copy.wait()
        if t < 7:
            slots[(t + 1) % 2][...] = dot(left[...], t_ref[t + 1])
        middle[32 * t : 32 * t + 32, :] = turn_and_sum(slots[t % 2], wave1_ref, t)
    waves.wait()
    kept = [
        pltpu.make_async_copy(t_ref.at[4 * x2 + place[2]], last_ref.at[x2], sems.at[9 + x2]) for x2 in range(2)
    ]
    for copy in kept:
        copy.start()
    left[...] = dot(turn_ref[...], middle[...]).astype(BF)

    even[...] = dot(left[...], t_ref[0])
    for t in range(8):
        if t < 7:
            slots[(t + 1) % 2][...] = dot(left[...], t_ref[t + 1])
        value = turn_and_sum(slots[t % 2], wave2_ref, t)
        value = jnp.concatenate([value[:, :HALF], value[:, HALF:]], axis=0)
        value = dot(leave_ref[...], value)
        for t4 in range(8):
            out_ref[t4, t] = value[8 * t4 : 8 * t4 + 8].astype(BF)
    for copy in kept:
        copy.wait()


def levels(place, share, translation, wave1, wave2):
    vmem, hbm = pl.BlockSpec(memory_space=pltpu.VMEM), pl.BlockSpec(memory_space=pl.ANY)
    return pl.pallas_call(
        levels_kernel,
        out_shape=[
            jax.ShapeDtypeStruct((8, 8, 8, HALF), BF),
            jax.ShapeDtypeStruct((2, CHEB, CHEB), BF),
        ],
        in_specs=[pl.BlockSpec(memory_space=pltpu.SMEM), vmem, hbm, vmem, hbm, vmem, vmem, vmem],
        out_specs=[vmem, vmem],
        scratch_shapes=[
            pltpu.VMEM((8, CHEB, CHEB), BF),
            pltpu.VMEM((8, 2, 64, CHEB), F32),
            pltpu.VMEM((256, CHEB), BF),
            pltpu.VMEM((256, CHEB), BF),
            pltpu.VMEM((256, CHEB), F32),
            pltpu.VMEM((256, CHEB), F32),
            pltpu.SemaphoreType.DMA((11,)),
        ],
        compiler_params=params(20),
        name="levels",
    )(
        place,
        share,
        in_hbm(translation),
        wave1,
        in_hbm(wave2),
        jnp.asarray(ENTER, BF),
        jnp.asarray(TURN, BF),
        jnp.asarray(LEAVE, BF),
    )


def final_kernel(place, n0, n1, n2, n3, pick_ref, t_ref, out_ref, left, made, sems):
    own = place[2]
    copies = []
    for group in range(2):
        for block in range(2 * group, 2 * group + 2):
            for high in range(2):
                at = 128 * block + 64 * high
                held = jnp.concatenate([r[at : at + 64] for r in (n0, n1, n2, n3)], axis=0)
                value = dot(pick_ref[own], held)
                value = jnp.concatenate([value[:128], value[128:]], axis=1)
                left[256 * block + 128 * high : 256 * block + 128 * high + 128, :] = value.astype(BF)
        rows = slice(512 * group, 512 * group + 512)
        for x2 in range(2):
            made[x2, rows] = dot(left[rows], t_ref[x2]).astype(BF)
            copies.append(
                pltpu.make_async_copy(made.at[x2, rows], out_ref.at[x2, rows], sems.at[x2, group])
            )
            copies[-1].start()
    for copy in copies:
        copy.wait()


def final(place, near, last):
    vmem = pl.BlockSpec(memory_space=pltpu.VMEM)
    return pl.pallas_call(
        final_kernel,
        out_shape=jax.ShapeDtypeStruct((2, 1024, CHEB), BF),
        in_specs=[pl.BlockSpec(memory_space=pltpu.SMEM)] + [vmem] * 6,
        out_specs=pl.BlockSpec(memory_space=pl.ANY),
        scratch_shapes=[
            pltpu.VMEM((1024, CHEB), BF),
            pltpu.VMEM((2, 1024, CHEB), BF),
            pltpu.SemaphoreType.DMA((2, 4)),
        ],
        compiler_params=params(14),
        name="final",
    )(place, *near, jnp.asarray(FINAL, BF), last)


def swap(value, axis):
    return lax.ppermute(value, axis, [(0, 1), (1, 0)])


def four(value):
    other = swap(value, "y2")
    return value, swap(value, "z2"), other, swap(other, "z2")


def exchange(value, axes):
    return lax.all_to_all(value, axes, split_axis=0, concat_axis=0, tiled=True)


def shards(weights, angles, translation):
    bit = lax.axis_index
    place = jnp.stack([bit("y4"), bit("z4"), 2 * bit("y2") + bit("z2")]).astype(jnp.int32)
    shape = weights.shape
    weights = in_hbm(weights.reshape(2, 4, 256, CHEB))
    angles = in_hbm(angles.reshape(3, 2, 4, 4, 4, CHEB))
    send0, send1, keep0, keep1, phases = rotate(place, weights, angles)
    come0, come1 = swap(send0, "y4"), swap(send1, "z4")
    phases = exchange(phases.reshape(64, 8, HALF), ("x4", "y4", "z4", "x3", "y3", "z3"))
    again0, again1 = first_sum(keep0, come0), first_sum(keep1, come1)
    again0, again1 = swap(again0, "z4"), swap(again1, "y4")
    share = sums(keep0, come0, again0, keep1, come1, again1)
    phases, _ = lax.optimization_barrier((phases, share))
    near = four(phases.reshape(8, 64, HALF))
    share = exchange(share.reshape(64, 8, CHEB), ("x4", "x3", "y3", "z3", "y2", "z2"))
    wave1, wave2 = trig(place, near)
    done, last = levels(place, share.reshape(2, 256, CHEB), translation, wave1, wave2)
    done = exchange(done.reshape(64, 8, HALF), ("y4", "z4", "x4", "x3", "y3", "z3"))
    near = four(done.reshape(512, HALF))
    return final(place, near, last).reshape(shape)


def solution(mesh):
    fine = Mesh(mesh.devices.reshape((2,) * len(BITS)), BITS)
    x, y, z = BITS[:2], BITS[2:5], BITS[5:]
    return jax.shard_map(
        shards,
        mesh=fine,
        in_specs=(P(x, y, z, None, None, None), P(None, x, y, z, None), P()),
        out_specs=P(x, y, z, None, None, None),
        check_vma=False,
    )
```

```python
import jax
import jax.numpy as jnp
import numpy as np
from jax import lax
from jax.experimental import pallas as pl
from jax.experimental.pallas import tpu as pltpu
from jax.sharding import Mesh
from jax.sharding import PartitionSpec as P

BITS = ("x4", "x3", "y4", "y3", "y2", "z4", "z3", "z2")
CHEB = 512
HALF = 256
BF = jnp.bfloat16
F32 = jnp.float32

SIN = (1.0, -0.1666666567325592, 0.00833332072943449, -0.00019840527966152877, 2.753572516667191e-06,
       -2.472758353633253e-08, 1.3608578153245787e-10)
COS = (1.0, -0.49999988079071045, 0.04166648909449577, -0.0013887794921174645, 2.4769700758042745e-05,
       -2.707722615014063e-07, 1.7238451777146224e-09)


def sin_cos(angle):
    square = angle * angle
    sine, cosine = jnp.full_like(square, SIN[-1]), jnp.full_like(square, COS[-1])
    for s, c in zip(SIN[-2::-1], COS[-2::-1]):
        sine, cosine = sine * square + s, cosine * square + c
    return sine * angle, cosine


def selection(source, count):
    source = np.asarray(source).reshape(-1)
    matrix = np.zeros((source.size, count), np.float32)
    matrix[np.arange(source.size), source] = 1
    return matrix


def rows(dims, order):
    return np.arange(int(np.prod(dims))).reshape(dims).transpose(order)


MIX = selection(rows((2, 8, 2, 4, 2), (1, 3, 0, 2, 4)), 256)
SEND_PHASE = selection(rows((2, 2, 2, 16), (3, 1, 2, 0)), 128)
ENTER = selection(rows((8, 4, 2, 2, 2), (0, 3, 4, 1, 2)), 256)
TURN = selection(rows((8, 2, 2, 8), (3, 1, 2, 0)), 256)
LEAVE = selection(rows((2, 2, 2, 2, 2, 2), (4, 5, 3, 1, 2, 0)), 64)


def phase_picks():
    first, second = [], []
    at = np.arange(256).reshape(4, 8, 2, 2, 2)
    for own in range(4):
        near = at[[yz ^ own for yz in range(4)]]
        first.append(selection(near[:, :, 0].transpose(3, 1, 0, 2), 256))
        second.append(selection(near[:, :, 1].transpose(3, 0, 2, 1), 256))
    return np.stack(first), np.stack(second)


def final_picks():
    at = np.arange(256).reshape(4, 8, 2, 2, 2)
    return np.stack(
        [
            selection(at[[yz ^ own for yz in range(4)]].transpose(4, 1, 2, 0, 3), 256)
            for own in range(4)
        ]
    )


FIRST, SECOND = phase_picks()
FINAL = final_picks()


def dot(a, b):
    return jnp.dot(a, b, preferred_element_type=F32)


def in_hbm(value):
    return pltpu.with_memory_space_constraint(value, pltpu.HBM)


def params(mebibytes):
    return pltpu.CompilerParams(vmem_limit_bytes=mebibytes * 1024 * 1024)


def rotate_kernel(place, w_hbm, a_hbm, mix_hbm, order_hbm, send0, send1, keep0, keep1, phases,
                  w_ref, a_ref, mix_ref, order_ref, waves, mixed, far, w_sems, sems):
    blocks = []
    for z, y, high in ((0, 0, 0), (1, 0, 0), (0, 0, 1), (0, 1, 1), (0, 1, 0), (1, 1, 0), (1, 0, 1), (1, 1, 1)):
        blocks.append(((place[0] ^ (1 - y)) * 2 + (place[1] ^ (1 - z)), high))
    small = [pltpu.make_async_copy(a_hbm.at[0], a_ref.at[0], sems.at[0])]
    small.append(pltpu.make_async_copy(mix_hbm, mix_ref, sems.at[1]))
    small.append(pltpu.make_async_copy(a_hbm.at[1:3], a_ref.at[1:3], sems.at[2]))
    small.append(pltpu.make_async_copy(order_hbm, order_ref, sems.at[3]))
    large = [
        pltpu.make_async_copy(w_hbm.at[:, at, 128 * high : 128 * high + 128], w_ref.at[j], w_sems.at[j])
        for j, (at, high) in enumerate(blocks)
    ]
    small[0].start()
    large[0].start()
    small[1].start()
    for copy in large[1:]:
        copy.start()
    small[2].start()
    small[3].start()
    small[0].wait()
    small[2].wait()
    small[3].wait()
    for j, (at, high) in enumerate(blocks):
        for x2 in range(2):
            for y in range(2):
                waves[j, x2, 0, 4 * y : 4 * y + 4, :] = a_ref[0, x2, at, 2 * high + y]
            sine, cosine = sin_cos(waves[j, x2, 0])
            waves[j, x2, 0] = sine
            waves[j, x2, 1] = cosine
    for j, (at, high) in enumerate(blocks):
        if j == 0:
            for copy in large:
                copy.wait()
            small[1].wait()
        for x2 in range(2):
            sine, cosine = waves[j, x2, 0], waves[j, x2, 1]
            for low in range(8):
                block = w_ref[j, x2, 16 * low : 16 * low + 16, :].astype(F32)
                re, im = block[:8], block[8:]
                s = sine[low : low + 1]
                c = cosine[low : low + 1]
                turned = jnp.concatenate([re * c - im * s, re * s + im * c], axis=0)
                row = 128 * x2 + 16 * low
                mixed[j, row : row + 16, :] = turned.astype(BF)
        (send0, send1, keep0, keep1)[j // 2][j % 2] = dot(mix_ref[...], mixed[j]).astype(BF)
    for block in range(4):
        for level in range(2):
            for x2 in range(2):
                for y in range(4):
                    row = 32 * level + 16 * x2 + 4 * y
                    far[block, row : row + 4, :] = a_ref[1 + level, x2, block, y]
        value = far[block].astype(BF)
        value = jnp.concatenate([value[:, :HALF], value[:, HALF:]], axis=0)
        value = dot(order_ref[...], value).astype(BF)
        for high in range(2):
            phases[high, block] = value[64 * high : 64 * high + 64]


def rotate(place, weights, angles):
    piece = jax.ShapeDtypeStruct((2, 256, CHEB), BF)
    return pl.pallas_call(
        rotate_kernel,
        out_shape=[piece] * 4 + [jax.ShapeDtypeStruct((2, 4, 64, HALF), BF)],
        in_specs=[pl.BlockSpec(memory_space=pltpu.SMEM)] + [pl.BlockSpec(memory_space=pl.ANY)] * 4,
        out_specs=[pl.BlockSpec(memory_space=pltpu.VMEM)] * 5,
        scratch_shapes=[
            pltpu.VMEM((8, 2, 128, CHEB), BF),
            pltpu.VMEM((3, 2, 4, 4, 4, CHEB), F32),
            pltpu.VMEM((256, 256), BF),
            pltpu.VMEM((128, 128), BF),
            pltpu.VMEM((8, 2, 2, 8, CHEB), F32),
            pltpu.VMEM((8, 256, CHEB), BF),
            pltpu.VMEM((4, 64, CHEB), F32),
            pltpu.SemaphoreType.DMA((8,)),
            pltpu.SemaphoreType.DMA((4,)),
        ],
        compiler_params=params(16),
        name="rotate",
    )(place, weights, angles, in_hbm(jnp.asarray(MIX, BF)), in_hbm(jnp.asarray(SEND_PHASE, BF)))


def add(a, b):
    return (a.astype(F32) + b.astype(F32)).astype(BF)


def part_kernel(part):
    def kernel(kept, come, out_ref):
        out_ref[...] = add(kept[part], come[part])

    return kernel


def part_sum(kept, come, part):
    return pl.pallas_call(
        part_kernel(part),
        out_shape=jax.ShapeDtypeStruct((256, CHEB), BF),
        in_specs=[pl.BlockSpec(memory_space=pltpu.VMEM)] * 2,
        out_specs=pl.BlockSpec(memory_space=pltpu.VMEM),
        compiler_params=params(8),
        name=f"part_sum{part}",
    )(kept, come)


def sum_kernel(kept0, again0, kept1, again1, out_ref):
    out_ref[0] = add(kept0[...], again0[...])
    out_ref[1] = add(kept1[...], again1[...])


def sums(*args):
    return pl.pallas_call(
        sum_kernel,
        out_shape=jax.ShapeDtypeStruct((2, 256, CHEB), BF),
        in_specs=[pl.BlockSpec(memory_space=pltpu.VMEM)] * 4,
        out_specs=pl.BlockSpec(memory_space=pltpu.VMEM),
        compiler_params=params(8),
        name="sums",
    )(*args)


def trig_kernel(place, *refs):
    near1, near2 = refs[0:4], refs[4:8]
    first_ref, second_ref, out1_ref, out2_ref = refs[8:]
    step = pl.program_id(0)

    def write(out_ref, t, angle):
        for half in range(2):
            for at in range(0, 64, 8):
                sine, cosine = sin_cos(angle[64 * half + at : 64 * half + at + 8])
                out_ref[t, 0, at : at + 8, HALF * half : HALF * half + HALF] = sine
                out_ref[t, 1, at : at + 8, HALF * half : HALF * half + HALF] = cosine

    @pl.when(step < 2)
    def _():
        for t in range(4):
            held = jnp.concatenate([r[t] for r in near1], axis=0)
            write(out1_ref, t, dot(first_ref[0], held))

    @pl.when(step >= 2)
    def _():
        for t in range(4):
            held = [r[:, 8 * t : 8 * t + 8, :].astype(F32).reshape(64, HALF) for r in near2]
            write(out2_ref, t, dot(second_ref[0], jnp.concatenate(held, axis=0).astype(BF)))


def trig(place, near):
    def own(*shape):
        return pl.BlockSpec((1, *shape), lambda i, p: (p[2],) + (0,) * len(shape))

    spec = pltpu.PrefetchScalarGridSpec(
        num_scalar_prefetch=1,
        grid=(4,),
        in_specs=[pl.BlockSpec((4, 64, HALF), lambda i, p: (jnp.minimum(i, 1), 0, 0))] * 4
        + [pl.BlockSpec((8, 32, HALF), lambda i, p: (0, jnp.maximum(i - 2, 0), 0))] * 4
        + [own(128, 256), own(128, 256)],
        out_specs=[
            pl.BlockSpec((4, 2, 64, CHEB), lambda i, p: (jnp.minimum(i, 1), 0, 0, 0)),
            pl.BlockSpec((4, 2, 64, CHEB), lambda i, p: (jnp.maximum(i - 2, 0), 0, 0, 0)),
        ],
    )
    return pl.pallas_call(
        trig_kernel,
        grid_spec=spec,
        out_shape=[jax.ShapeDtypeStruct((8, 2, 64, CHEB), F32), pltpu.HBM((8, 2, 64, CHEB), F32)],
        compiler_params=params(14),
        cost_estimate=pl.CostEstimate(flops=7 * 10**9, bytes_accessed=10**6, transcendentals=0),
        name="trig",
    )(place, *near, *near, in_hbm(jnp.asarray(FIRST, BF)), in_hbm(jnp.asarray(SECOND, BF)))


def levels_kernel(place, x_ref, t_hbm, wave1_ref, wave2_hbm, enter_ref, turn_ref, leave_ref, out_ref, last_ref,
                  t_ref, wave2_ref, left, middle, even, odd, sems):
    matrices = [pltpu.make_async_copy(t_hbm.at[t], t_ref.at[t], sems.at[t]) for t in range(8)]
    waves = pltpu.make_async_copy(wave2_hbm, wave2_ref, sems.at[8])
    for copy in matrices:
        copy.start()
    waves.start()
    total = (x_ref[0].astype(F32) + x_ref[1].astype(F32)).astype(BF)
    left[...] = dot(enter_ref[...], total).astype(BF)

    def turn_and_sum(product, wave_ref, at):
        total = [jnp.zeros((8, CHEB), F32)] * 4
        for outer in range(8):
            sine = wave_ref[at, 0, 8 * outer : 8 * outer + 8, :]
            cosine = wave_ref[at, 1, 8 * outer : 8 * outer + 8, :]
            for r in range(2):
                row = 32 * outer + 8 * r
                re = product[row : row + 8, :]
                im = product[row + 16 : row + 24, :]
                total[r] = total[r] + (re * cosine - im * sine)
                total[2 + r] = total[2 + r] + (re * sine + im * cosine)
        return jnp.concatenate(total, axis=0).astype(BF)

    slots = (even, odd)
    for copy in matrices[:2]:
        copy.wait()
    even[...] = dot(left[...], t_ref[0])
    for t in range(8):
        if t % 2 == 1:
            for copy in matrices[t + 1 : t + 3]:
                copy.wait()
        if t < 7:
            slots[(t + 1) % 2][...] = dot(left[...], t_ref[t + 1])
        middle[32 * t : 32 * t + 32, :] = turn_and_sum(slots[t % 2], wave1_ref, t)
    waves.wait()
    kept = [
        pltpu.make_async_copy(t_ref.at[4 * x2 + place[2]], last_ref.at[x2], sems.at[9 + x2]) for x2 in range(2)
    ]
    for copy in kept:
        copy.start()
    left[...] = dot(turn_ref[...], middle[...]).astype(BF)

    even[...] = dot(left[...], t_ref[0])
    for t in range(8):
        if t < 7:
            slots[(t + 1) % 2][...] = dot(left[...], t_ref[t + 1])
        value = turn_and_sum(slots[t % 2], wave2_ref, t)
        value = jnp.concatenate([value[:, :HALF], value[:, HALF:]], axis=0)
        value = dot(leave_ref[...], value)
        for t4 in range(8):
            out_ref[t4, t] = value[8 * t4 : 8 * t4 + 8].astype(BF)
    for copy in kept:
        copy.wait()


def levels(place, share, translation, wave1, wave2):
    vmem, hbm = pl.BlockSpec(memory_space=pltpu.VMEM), pl.BlockSpec(memory_space=pl.ANY)
    return pl.pallas_call(
        levels_kernel,
        out_shape=[
            jax.ShapeDtypeStruct((8, 8, 8, HALF), BF),
            jax.ShapeDtypeStruct((2, CHEB, CHEB), BF),
        ],
        in_specs=[pl.BlockSpec(memory_space=pltpu.SMEM), vmem, hbm, vmem, hbm, vmem, vmem, vmem],
        out_specs=[vmem, vmem],
        scratch_shapes=[
            pltpu.VMEM((8, CHEB, CHEB), BF),
            pltpu.VMEM((8, 2, 64, CHEB), F32),
            pltpu.VMEM((256, CHEB), BF),
            pltpu.VMEM((256, CHEB), BF),
            pltpu.VMEM((256, CHEB), F32),
            pltpu.VMEM((256, CHEB), F32),
            pltpu.SemaphoreType.DMA((11,)),
        ],
        compiler_params=params(20),
        name="levels",
    )(
        place,
        share,
        in_hbm(translation),
        wave1,
        in_hbm(wave2),
        jnp.asarray(ENTER, BF),
        jnp.asarray(TURN, BF),
        jnp.asarray(LEAVE, BF),
    )


def final_kernel(place, n0, n1, n2, n3, pick_ref, t_ref, out_ref, left, made, sems):
    own = place[2]
    copies = []
    for group in range(2):
        for block in range(2 * group, 2 * group + 2):
            for high in range(2):
                at = 128 * block + 64 * high
                held = jnp.concatenate([r[at : at + 64] for r in (n0, n1, n2, n3)], axis=0)
                value = dot(pick_ref[own], held)
                value = jnp.concatenate([value[:128], value[128:]], axis=1)
                left[256 * block + 128 * high : 256 * block + 128 * high + 128, :] = value.astype(BF)
        rows = slice(512 * group, 512 * group + 512)
        for x2 in range(2):
            made[x2, rows] = dot(left[rows], t_ref[x2]).astype(BF)
            copies.append(
                pltpu.make_async_copy(made.at[x2, rows], out_ref.at[x2, rows], sems.at[x2, group])
            )
            copies[-1].start()
    for copy in copies:
        copy.wait()


def final(place, near, last):
    vmem = pl.BlockSpec(memory_space=pltpu.VMEM)
    return pl.pallas_call(
        final_kernel,
        out_shape=jax.ShapeDtypeStruct((2, 1024, CHEB), BF),
        in_specs=[pl.BlockSpec(memory_space=pltpu.SMEM)] + [vmem] * 6,
        out_specs=pl.BlockSpec(memory_space=pl.ANY),
        scratch_shapes=[
            pltpu.VMEM((1024, CHEB), BF),
            pltpu.VMEM((2, 1024, CHEB), BF),
            pltpu.SemaphoreType.DMA((2, 4)),
        ],
        compiler_params=params(14),
        name="final",
    )(place, *near, jnp.asarray(FINAL, BF), last)


def swap(value, axis):
    return lax.ppermute(value, axis, [(0, 1), (1, 0)])


def four(value):
    other = swap(value, "y2")
    return value, swap(value, "z2"), other, swap(other, "z2")


def exchange(value, axes):
    return lax.all_to_all(value, axes, split_axis=0, concat_axis=0, tiled=True)


def shards(weights, angles, translation):
    bit = lax.axis_index
    place = jnp.stack([bit("y4"), bit("z4"), 2 * bit("y2") + bit("z2")]).astype(jnp.int32)
    shape = weights.shape
    weights = in_hbm(weights.reshape(2, 4, 256, CHEB))
    angles = in_hbm(angles.reshape(3, 2, 4, 4, 4, CHEB))
    send0, send1, keep0, keep1, phases = rotate(place, weights, angles)
    come0, come1 = swap(send0, "y4"), swap(send1, "z4")
    phases = exchange(phases.reshape(64, 8, HALF), ("x4", "y4", "z4", "x3", "y3", "z3"))
    again0, again1 = part_sum(keep0, come0, 0), part_sum(keep1, come1, 0)
    again0, again1 = swap(again0, "z4"), swap(again1, "y4")
    share = sums(part_sum(keep0, come0, 1), again0, part_sum(keep1, come1, 1), again1)
    phases, _ = lax.optimization_barrier((phases, share))
    near = four(phases.reshape(8, 64, HALF))
    share = exchange(share.reshape(64, 8, CHEB), ("x4", "x3", "y3", "z3", "y2", "z2"))
    wave1, wave2 = trig(place, near)
    done, last = levels(place, share.reshape(2, 256, CHEB), translation, wave1, wave2)
    done = exchange(done.reshape(64, 8, HALF), ("y4", "z4", "x4", "x3", "y3", "z3"))
    near = four(done.reshape(512, HALF))
    return final(place, near, last).reshape(shape)


def solution(mesh):
    fine = Mesh(mesh.devices.reshape((2,) * len(BITS)), BITS)
    x, y, z = BITS[:2], BITS[2:5], BITS[5:]
    return jax.shard_map(
        shards,
        mesh=fine,
        in_specs=(P(x, y, z, None, None, None), P(None, x, y, z, None), P()),
        out_specs=P(x, y, z, None, None, None),
        check_vma=False,
    )
```
